32 devices in a mesh: groups: 2 (over y), seq: 16 (over z, x, core).
Axes of the slice: x: 2, y: 2, z: 4, core: 2. Of those that a mesh axis runs over, the one named last changes fastest.
Arguments:
- inputs: bfloat16 [4, 8192, 1536], P('groups', 'seq'), parts along dimension 0, may hold values from -6 to 6
- conv_weight: bfloat16 [3, 1536, 768], P(None, 'seq'), may hold values from -0.09375 to 0.09375
- proj_weight: bfloat16 [1536, 768], P('seq'), may hold values from -0.21875 to 0.21875
- cotangent: bfloat16 [4, 8192, 1536], P('groups', 'seq'), parts along dimension 0, may hold values from -6 to 6
Outputs:
- outputs: bfloat16 [4, 8192, 1536], P('groups', 'seq'), parts along dimension 0
- input_grad: bfloat16 [4, 8192, 1536], P('groups', 'seq'), parts along dimension 0
- conv_grad: float32 [3072, 3, 768], P(('groups', 'seq')), parts along dimension 0
- proj_grad: float32 [3072, 768], P(('groups', 'seq')), parts along dimension 0
The draws below stay inside these ranges and needn't reach their ends.
There are 2 independent parts, one for each index of `groups`. The reference program is written for one: setup_inputs(seed, part) draws one part's arguments, and reference() takes and returns one part's arrays. A program takes and returns all parts, laid end to end along the dimension named above; an argument that names none is the same for every part. Nothing has to cross between parts.
All inputs are finite; a program needn't handle non-finite values.
Results may differ from the reference program's by a relative error of at most 0.0051.
Values may be sent and summed in bfloat16 or wider, within the bound.
A program may use at most 128 MiB of HBM per device.

```python
import jax
import jax.numpy as jnp

C = 1536
H = 768
L = 8192
B = 2


def spiked(array, stream_key, source, target, blocks, factor):
    def block_of(dim):
        return (jnp.arange(array.shape[dim]) // (array.shape[dim] // blocks)).reshape((-1,) + (1,) * (array.ndim - 1 - dim))

    first = jax.random.permutation(stream_key, blocks)[block_of(target)]
    far = (block_of(target) + blocks // 2) % blocks
    return jnp.where((block_of(source) == first) | (block_of(source) == far), factor * array, array)


def block_scale(own_key, shape, pieces, least, high):
    def one(dim, blocks):
        heights = jax.random.uniform(jax.random.fold_in(jax.random.fold_in(own_key, 6), dim), (blocks,), jnp.float32, least / len(pieces), high / len(pieces))
        return jnp.repeat(jnp.exp(heights), shape[dim] // blocks).reshape((-1,) + (1,) * (len(shape) - dim - 1))

    gain = one(*pieces[0])
    for cut in pieces[1:]:
        gain = gain * one(*cut)
    return gain


def normal_values(stream_key, extent, spread, limit, pieces=(), kind=jnp.bfloat16):
    level = block_scale(stream_key, extent, pieces, -0.22, 0.18) if pieces else 1.0
    result = jax.random.normal(stream_key, extent, jnp.float32) * spread * level
    return jnp.minimum(jnp.maximum(result, -limit), limit).astype(kind)


def heavy_noise(rng, extent, deviation, bound, pieces, heavy, dtype=jnp.bfloat16):
    array = deviation * jax.random.normal(rng, extent, jnp.float32)
    if pieces:
        array = array * block_scale(rng, extent, pieces, -0.22, 0.18)
    return jnp.clip(spiked(array, jax.random.fold_in(rng, 3), *heavy), -bound, bound).astype(dtype)


def setup_inputs(seed: int = 0, part: int = 0) -> dict:
    arg_keys = jax.random.split(jax.random.key(seed), 5)
    own_keys = jax.random.split(jax.random.fold_in(arg_keys[4], part), 5)
    return {
        "inputs": heavy_noise(own_keys[0], (B, L, C), 1.0, 6.0, ((1, 16),), (1, 2, 16, 2.0)),
        "conv_weight": normal_values(arg_keys[1], (3, C, H), (3 * C) ** -0.5, 0.09375, ((1, 16),)),
        "proj_weight": normal_values(arg_keys[2], (C, H), H ** -0.5, 0.21875, ((0, 16),)),
        "cotangent": heavy_noise(own_keys[3], (B, L, C), 1.0, 6.0, ((1, 16),), (1, 2, 16, 2.0)),
    }


def shift_rows(values, offset):
    width = values.shape[1]
    if offset > 0:
        padded = jnp.pad(values, ((0, 0), (0, offset), (0, 0)))
        return padded[:, offset:offset + width, :]
    if offset < 0:
        padded = jnp.pad(values, ((0, 0), (-offset, 0), (0, 0)))
        return padded[:, :width, :]
    return values

def gelu_grad(point, upstream):
    return jax.vjp(jax.nn.gelu, point)[1](upstream)[0]

def reference(inputs, conv_weight, proj_weight, cotangent):
    dilation = L // 8
    batch = inputs.shape[0]
    chans = inputs.shape[2]
    hid = conv_weight.shape[2]
    scale = 1.0 / float(batch * L) ** 0.5
    acted = jax.nn.gelu(inputs.astype(jnp.float32)).astype(jnp.bfloat16)
    hidden = jnp.zeros((batch * L, hid), jnp.float32)
    for k in range(3):
        moved = shift_rows(acted, (k - 1) * dilation).reshape(-1, chans)
        hidden = hidden + jnp.dot(moved, conv_weight[k], preferred_element_type=jnp.float32)
    gated = jax.nn.gelu(hidden).astype(jnp.bfloat16)
    outputs = (inputs.reshape(-1, chans).astype(jnp.float32) + jnp.dot(gated, proj_weight.T, preferred_element_type=jnp.float32)).astype(jnp.bfloat16)
    cot_rows = cotangent.reshape(-1, chans)
    gated_grad = jnp.dot(cot_rows, proj_weight, preferred_element_type=jnp.float32)
    hidden_grad = gelu_grad(hidden, gated_grad).astype(jnp.bfloat16)
    grad_blocks = hidden_grad.reshape(batch, L, hid)
    acted_grad = jnp.zeros((batch * L, chans), jnp.float32)
    kernel_parts = []
    for k in range(3):
        moved_grad = shift_rows(grad_blocks, -(k - 1) * dilation).reshape(-1, hid)
        acted_grad = acted_grad + jnp.dot(moved_grad, conv_weight[k].T, preferred_element_type=jnp.float32)
        moved = shift_rows(acted, (k - 1) * dilation).reshape(-1, chans)
        kernel_parts.append(jnp.dot(moved.T, hidden_grad, preferred_element_type=jnp.float32))
    input_grad = (cot_rows.astype(jnp.float32) + gelu_grad(inputs.reshape(-1, chans).astype(jnp.float32), acted_grad)).astype(jnp.bfloat16)
    conv_grad = jnp.stack(kernel_parts, axis=1) * scale
    proj_grad = jnp.dot(cot_rows.T, gated, preferred_element_type=jnp.float32) * scale
    return (outputs.reshape(batch, L, chans), input_grad.reshape(batch, L, chans), conv_grad, proj_grad)
```

```python
import functools

import jax
import jax.numpy as jnp
from jax import lax
from jax.experimental import pallas as pl
from jax.experimental.pallas import tpu as pltpu
from jax.sharding import PartitionSpec as P

L = 8192


def from_behind(block, axis, distance):
    devices = range(lax.axis_size(axis))
    route = [(i - distance, i) for i in devices if i - distance in devices]
    return lax.ppermute(block, axis, route)


def gelu_grad(point, upstream):
    return jax.vjp(jax.nn.gelu, point)[1](upstream)[0]


def shards(inputs, conv_weight, proj_weight, cotangent):
    batch, local_len, chans = inputs.shape
    devices = lax.axis_size("seq")
    stride = devices // 8
    scale = 1.0 / float(batch * L) ** 0.5
    acted = jax.nn.gelu(inputs.astype(jnp.float32)).astype(jnp.bfloat16)
    conv_weight, proj_weight = (
        lax.all_gather(conv_weight, "seq", axis=1, tiled=True),
        lax.all_gather(proj_weight, "seq", axis=0, tiled=True),
    )
    hid = conv_weight.shape[2]
    acted_rows = acted.reshape(-1, chans)
    before = from_behind(acted, "seq", stride)
    after = from_behind(acted, "seq", -stride)
    hidden = jnp.dot(before.reshape(-1, chans), conv_weight[0], preferred_element_type=jnp.float32)
    hidden = hidden + jnp.dot(acted_rows, conv_weight[1], preferred_element_type=jnp.float32)
    hidden = hidden + jnp.dot(
        after.reshape(-1, chans), conv_weight[2], preferred_element_type=jnp.float32
    )
    gated = jax.nn.gelu(hidden).astype(jnp.bfloat16)
    outputs = (
        inputs.reshape(-1, chans).astype(jnp.float32)
        + jnp.dot(gated, proj_weight.T, preferred_element_type=jnp.float32)
    ).astype(jnp.bfloat16)
    cot_rows = cotangent.reshape(-1, chans)
    gated_grad = jnp.dot(cot_rows, proj_weight, preferred_element_type=jnp.float32)
    hidden_grad = gelu_grad(hidden, gated_grad).astype(jnp.bfloat16)
    grad_blocks = hidden_grad.reshape(batch, local_len, hid)
    grad_later = from_behind(grad_blocks, "seq", -stride).reshape(-1, hid)
    grad_earlier = from_behind(grad_blocks, "seq", stride).reshape(-1, hid)
    acted_grad = jnp.dot(grad_later, conv_weight[0].T, preferred_element_type=jnp.float32)
    acted_grad = acted_grad + jnp.dot(
        hidden_grad, conv_weight[1].T, preferred_element_type=jnp.float32
    )
    acted_grad = acted_grad + jnp.dot(
        grad_earlier, conv_weight[2].T, preferred_element_type=jnp.float32
    )
    input_grad = (
        cot_rows.astype(jnp.float32)
        + gelu_grad(inputs.reshape(-1, chans).astype(jnp.float32), acted_grad)
    ).astype(jnp.bfloat16)
    tap_grads = (grad_later, hidden_grad, grad_earlier)
    share = chans // devices
    local_terms = [
        jnp.dot(acted_rows.T, piece, preferred_element_type=jnp.float32) for piece in tap_grads
    ]
    local_terms.append(jnp.dot(cot_rows.T, gated, preferred_element_type=jnp.float32))
    stacked = jnp.stack(local_terms, axis=1)
    received = lax.all_to_all(stacked, "seq", split_axis=0, concat_axis=0, tiled=True)
    summed = jnp.sum(received.reshape(devices, share, 4, received.shape[2]), axis=0)
    conv_sum = summed[:, 0:3, :]
    proj_sum = summed[:, 3, :]
    return (
        outputs.reshape(batch, local_len, chans),
        input_grad.reshape(batch, local_len, chans),
        conv_sum * scale,
        proj_sum * scale,
    )


F32 = jnp.float32
BF16 = jnp.bfloat16
MESH = pl.DeviceIdType.MESH
VMEM = pl.BlockSpec(memory_space=pltpu.VMEM)
HBM = pl.BlockSpec(memory_space=pl.ANY)
SEQ = 16
CHUNKS = 4
COEF = 0.7978845608028654
CUBE = 0.044715


def place():
    s = lax.axis_index("seq")
    return s // 4, (s // 2) % 2, s % 2


def index(z, x, core):
    return (z * 2 + x) * 2 + core


def copy_to(src, dst, send, recv, target):
    return pltpu.make_async_remote_copy(
        src_ref=src, dst_ref=dst, send_sem=send, recv_sem=recv,
        device_id={"seq": target}, device_id_type=MESH,
    )


def greet(targets):
    barrier = pltpu.get_barrier_semaphore()
    for target in targets:
        pl.semaphore_signal(barrier, inc=1, device_id={"seq": target}, device_id_type=MESH)
    pl.semaphore_wait(barrier, len(targets))


def gelu_parts(v):
    t = jnp.tanh(COEF * (v + CUBE * v * v * v))
    half = 0.5 * (1.0 + t)
    return half * v, half + (0.5 * COEF) * v * (1.0 - t * t) * (1.0 + (3.0 * CUBE) * v * v)


def params(cid, mib=56):
    return pltpu.CompilerParams(
        collective_id=cid, has_side_effects=True, vmem_limit_bytes=mib * 1024 * 1024
    )


def gather_kernel(w_ref, x_ref, full_ref, acted_ref, own_sem, zs, zr, xs, xr, cs, cr):
    z, x, core = place()
    share = w_ref.shape[1]
    zt = [lax.rem(z + d, 4) for d in range(4)]
    zf = [lax.rem(z + 4 - d, 4) for d in range(4)]

    def rows(zz, xx, cc):
        start = pl.multiple_of(index(zz, xx, cc) * share, share)
        return full_ref.at[:, pl.ds(start, share), :]

    greet([index(zt[d], x, core) for d in (1, 2, 3)]
          + [index(z, 1 - x, core), index(z, x, 1 - core)])
    mine = rows(z, x, core)
    copies = []
    for d in (1, 3, 2):
        copies.append(copy_to(w_ref, mine, zs.at[d], zr.at[d], index(zt[d], x, core)))
        copies[-1].start()
    zc = dict(zip((1, 3, 2), copies))

    def to_x(j, src):
        c = copy_to(src, rows(zf[j], x, core), xs.at[j], xr.at[j], index(z, 1 - x, core))
        c.start()
        return c

    def to_core(j, src, xx):
        c = copy_to(src, rows(zf[j % 4], xx, core), cs.at[j], cr.at[j], index(z, x, 1 - core))
        c.start()
        return c

    xc = {0: to_x(0, w_ref)}
    cc = {0: to_core(0, w_ref, x)}
    own = pltpu.make_async_copy(w_ref, mine, own_sem)
    own.start()

    tile = 64

    def act(i, carry):
        r = pl.ds(pl.multiple_of(i * tile, tile), tile)
        v = x_ref[r, :].astype(F32)
        t = jnp.tanh(COEF * (v + CUBE * v * v * v))
        acted_ref[r, :] = (0.5 * v * (1.0 + t)).astype(BF16)
        return carry

    lax.fori_loop(0, x_ref.shape[0] // tile, act, 0)

    def take_z(j):
        zc[j].wait_recv()
        src = rows(zf[j], x, core)
        xc[j] = to_x(j, src)
        cc[j] = to_core(j, src, x)

    def take_x(j):
        xc[j].wait_recv()
        cc[4 + j] = to_core(4 + j, rows(zf[j], 1 - x, core), 1 - x)

    take_z(1)
    take_z(3)
    take_x(0)
    take_z(2)
    take_x(1)
    take_x(3)
    take_x(2)
    for j in range(8):
        cc[j].wait_recv()
    own.wait()
    for j in (1, 2, 3):
        zc[j].wait_send()
    for j in range(4):
        xc[j].wait_send()
    for j in range(8):
        cc[j].wait_send()


def gather(w4, flat):
    taps, share, hid = w4.shape
    dma = pltpu.SemaphoreType.DMA
    return pl.pallas_call(
        gather_kernel,
        out_shape=(
            jax.ShapeDtypeStruct((taps, share * SEQ, hid), BF16),
            jax.ShapeDtypeStruct(flat.shape, BF16),
        ),
        in_specs=[HBM, VMEM],
        out_specs=(HBM, VMEM),
        scratch_shapes=[dma, dma((4,)), dma((4,)), dma((4,)), dma((4,)), dma((8,)), dma((8,))],
        compiler_params=params(0),
        name="gather_weights",
    )(w4, flat)


def forward_kernel(acted_ref, w_ref, cot_ref, gated_ref, hg_ref,
                   out_a, in_a, out_s, in_s, part, gg, zs, zr, xs, xr):
    z, x, core = place()
    up = x == 1
    sends = jnp.logical_or(jnp.logical_and(up, z < 3), jnp.logical_and(x == 0, z > 0))
    takes = jnp.logical_or(jnp.logical_and(up, z > 0), jnp.logical_and(x == 0, z < 3))
    step = 2 * x - 1
    ahead = index(lax.rem(z + step + 4, 4), x, core)
    behind = index(lax.rem(z - step + 4, 4), x, core)
    across = index(z, 1 - x, core)
    greet([ahead, behind, across])
    n = acted_ref.shape[0] // CHUNKS
    tap_far = 2 - 2 * x
    tap_near = 2 * x

    def rows(i):
        return pl.ds(pl.multiple_of(i * n, n), n)

    def z_copy(i):
        return copy_to(out_a.at[i], in_a.at[i], zs.at[i], zr.at[i], ahead)

    def x_copy(i):
        return copy_to(out_s.at[i], in_s.at[i], xs.at[i], xr.at[i], across)

    def far(i, carry):
        out_a[i] = jnp.dot(acted_ref[rows(i), :], w_ref[tap_far], preferred_element_type=F32).astype(BF16)

        @pl.when(sends)
        def _():
            z_copy(i).start()
        return carry

    lax.fori_loop(0, CHUNKS, far, 0)

    def near(i, carry):
        part[i] = jnp.dot(acted_ref[rows(i), :], w_ref[tap_near], preferred_element_type=F32)
        gg[i] = jnp.dot(cot_ref[rows(i), :], w_ref[3], preferred_element_type=F32)
        return carry

    lax.fori_loop(0, CHUNKS, near, 0)

    def combine(i, carry):
        @pl.when(takes)
        def _():
            z_copy(i).wait_recv()
            part[i] = part[i] + in_a[i].astype(F32)
        out_s[i] = part[i].astype(BF16)
        x_copy(i).start()
        part[i] = jnp.dot(acted_ref[rows(i), :], w_ref[1], preferred_element_type=F32)
        return carry

    lax.fori_loop(0, CHUNKS, combine, 0)

    def finish(i, carry):
        x_copy(i).wait_recv()
        hidden = part[i] + in_s[i].astype(F32)
        value, slope = gelu_parts(hidden)
        gated_ref[rows(i), :] = value.astype(BF16)
        hg_ref[rows(i), :] = (gg[i] * slope).astype(BF16)
        return carry

    lax.fori_loop(0, CHUNKS, finish, 0)

    def drain(i, carry):
        x_copy(i).wait_send()

        @pl.when(sends)
        def _():
            z_copy(i).wait_send()
        return carry

    lax.fori_loop(0, CHUNKS, drain, 0)


def forward(acted, w4, cot):
    m = acted.shape[0]
    hid = w4.shape[2]
    dma = pltpu.SemaphoreType.DMA
    block = (CHUNKS, m // CHUNKS, hid)
    return pl.pallas_call(
        forward_kernel,
        out_shape=(jax.ShapeDtypeStruct((m, hid), BF16),) * 2,
        in_specs=[VMEM] * 3,
        out_specs=(VMEM, VMEM),
        scratch_shapes=[pltpu.VMEM(block, BF16)] * 4 + [pltpu.VMEM(block, F32)] * 2
        + [dma((CHUNKS,))] * 4,
        compiler_params=params(1),
        name="forward_halo",
    )(acted, w4, cot)


def halo_kernel(hg_ref, later_ref, earlier_ref, from_x, from_z, zs, zr, xs, xr):
    z, x, core = place()
    even = x == 0
    sends = jnp.logical_or(jnp.logical_and(even, z < 3), jnp.logical_and(x == 1, z > 0))
    takes = jnp.logical_or(jnp.logical_and(even, z > 0), jnp.logical_and(x == 1, z < 3))
    step = 1 - 2 * x
    ahead = index(lax.rem(z + step + 4, 4), x, core)
    behind = index(lax.rem(z - step + 4, 4), x, core)
    across = index(z, 1 - x, core)
    greet([ahead, behind, across])
    n = hg_ref.shape[0] // CHUNKS

    def rows(i):
        return pl.ds(pl.multiple_of(i * n, n), n)

    def x_copy(i):
        return copy_to(hg_ref.at[rows(i), :], from_x.at[i], xs.at[i], xr.at[i], across)

    def z_copy(i):
        return copy_to(from_x.at[i], from_z.at[i], zs.at[i], zr.at[i], ahead)

    def launch(i, carry):
        x_copy(i).start()
        return carry

    lax.fori_loop(0, CHUNKS, launch, 0)

    def onward(i, carry):
        x_copy(i).wait_recv()

        @pl.when(sends)
        def _():
            z_copy(i).start()
        return carry

    lax.fori_loop(0, CHUNKS, onward, 0)

    def finish(i, carry):
        @pl.when(takes)
        def _():
            z_copy(i).wait_recv()

        @pl.when(jnp.logical_not(takes))
        def _():
            from_z[i] = jnp.zeros(from_z.shape[1:], BF16)

        @pl.when(even)
        def _():
            later_ref[rows(i), :] = from_x[i]
            earlier_ref[rows(i), :] = from_z[i]

        @pl.when(x == 1)
        def _():
            later_ref[rows(i), :] = from_z[i]
            earlier_ref[rows(i), :] = from_x[i]
        return carry

    lax.fori_loop(0, CHUNKS, finish, 0)

    def drain(i, carry):
        x_copy(i).wait_send()

        @pl.when(sends)
        def _():
            z_copy(i).wait_send()
        return carry

    lax.fori_loop(0, CHUNKS, drain, 0)


def halo(hg):
    m, hid = hg.shape
    dma = pltpu.SemaphoreType.DMA
    block = (CHUNKS, m // CHUNKS, hid)
    return pl.pallas_call(
        halo_kernel,
        out_shape=(jax.ShapeDtypeStruct((m, hid), BF16),) * 2,
        in_specs=[VMEM],
        out_specs=(VMEM, VMEM),
        scratch_shapes=[pltpu.VMEM(block, BF16)] * 2 + [dma((CHUNKS,))] * 4,
        compiler_params=params(2),
        name="backward_halo",
    )(hg)


ORDER = (2, 1, 3, 0)


def reduce_kernel(scale, acted_ref, cot_ref, later_ref, hg_ref, earlier_ref, gated_ref, out_ref,
                  give, keep, got, acc, x_out, x_in, z_out, z_in, cs, cr, xs, xr, zs, zr):
    z, x, core = place()
    share = out_ref.shape[1]
    zt = [lax.rem(z + d, 4) for d in range(4)]
    across = index(z, 1 - x, core)
    other = index(z, x, 1 - core)
    greet([index(zt[d], x, core) for d in (1, 2, 3)] + [across, other])
    taps = (later_ref, hg_ref, earlier_ref, gated_ref)
    wide = 4 * share
    tile = 256
    hid = hg_ref.shape[1]

    def core_copy(s):
        return copy_to(give.at[s % 2], got.at[s], cs.at[s], cr.at[s], other)

    def x_copy(s):
        return copy_to(x_out.at[s], x_in.at[s], xs.at[s], xr.at[s], across)

    def z_copy(s):
        return copy_to(z_out.at[s], z_in.at[s], zs.at[s], zr.at[s], index(zt[ORDER[s]], x, core))

    def compute(s):
        cols = pl.ds(pl.multiple_of(zt[ORDER[s]] * wide, wide), wide)
        for k in range(4):
            left = cot_ref if k == 3 else acted_ref

            def part(i, carry, k=k, left=left):
                t = pl.ds(pl.multiple_of(i * tile, tile), tile)
                p = lax.dot_general(left[:, cols], taps[k][:, t], (((0,), (0,)), ((), ())),
                                    preferred_element_type=F32)
                for xx in range(2):
                    lo = p[2 * xx * share:(2 * xx + 1) * share]
                    hi = p[(2 * xx + 1) * share:(2 * xx + 2) * share]
                    keep[s % 2, xx, k, :, t] = jnp.where(core == 0, lo, hi)
                    give[s % 2, xx, k, :, t] = jnp.where(core == 0, hi, lo)
                return carry

            lax.fori_loop(0, hid // tile, part, 0)
        core_copy(s).start()

    def to_across(s):
        core_copy(s).wait_recv()

        def add(k, carry):
            x_out[s, k] = (keep[s % 2, 1 - x, k] + got[s, 1 - x, k]).astype(BF16)
            acc[s, k] = keep[s % 2, x, k] + got[s, x, k]
            return carry

        lax.fori_loop(0, 4, add, 0)
        x_copy(s).start()

    def to_z(s):
        x_copy(s).wait_recv()

        def add(k, carry):
            z_out[s, k] = (acc[s, k] + x_in[s, k].astype(F32)).astype(BF16)
            return carry

        lax.fori_loop(0, 4, add, 0)
        z_copy(s).start()

    compute(0)
    compute(1)
    to_across(0)
    core_copy(0).wait_send()
    compute(2)
    to_across(1)
    core_copy(1).wait_send()
    compute(3)
    to_across(2)
    to_z(0)
    to_across(3)
    to_z(1)
    to_z(2)
    x_copy(3).wait_recv()
    for s in range(3):
        z_copy(s).wait_recv()

    def total(k, carry):
        own = acc[3, k] + x_in[3, k].astype(F32)
        for s in range(3):
            own = own + z_in[s, k].astype(F32)
        out_ref[k] = own * scale
        return carry

    lax.fori_loop(0, 4, total, 0)
    core_copy(2).wait_send()
    core_copy(3).wait_send()
    for s in range(4):
        x_copy(s).wait_send()
    for s in range(3):
        z_copy(s).wait_send()


def reduce_grads(scale, acted, cot, later, hg, earlier, gated):
    chans, hid = acted.shape[1], hg.shape[1]
    share = chans // SEQ
    dma = pltpu.SemaphoreType.DMA
    pair = (2, 4, share, hid)
    return pl.pallas_call(
        functools.partial(reduce_kernel, scale),
        out_shape=jax.ShapeDtypeStruct((4, share, hid), F32),
        in_specs=[VMEM] * 6,
        out_specs=VMEM,
        scratch_shapes=[
            pltpu.VMEM((2,) + pair, F32),
            pltpu.VMEM((2,) + pair, F32),
            pltpu.VMEM((4,) + pair, F32),
            pltpu.VMEM((4, 4, share, hid), F32),
            pltpu.VMEM((4, 4, share, hid), BF16),
            pltpu.VMEM((4, 4, share, hid), BF16),
            pltpu.VMEM((3, 4, share, hid), BF16),
            pltpu.VMEM((3, 4, share, hid), BF16),
            dma((4,)), dma((4,)), dma((4,)), dma((4,)), dma((3,)), dma((3,)),
        ],
        compiler_params=params(3),
        name="reduce_grads",
    )(acted, cot, later, hg, earlier, gated)


def pair_shards(inputs, conv_weight, proj_weight, cotangent):
    batch, local_len, chans = inputs.shape
    scale = 1.0 / float(batch * L) ** 0.5
    rows = inputs.reshape(-1, chans)
    cot = cotangent.reshape(-1, chans)
    full, acted = gather(jnp.concatenate([conv_weight, proj_weight[None]], axis=0), rows)
    gated, hg = forward(acted, full, cot)
    later, earlier = halo(hg)
    outputs = (
        rows.astype(F32) + jnp.dot(gated, full[3].T, preferred_element_type=F32)
    ).astype(BF16)
    acted_grad = jnp.dot(later, full[0].T, preferred_element_type=F32)
    acted_grad = acted_grad + jnp.dot(hg, full[1].T, preferred_element_type=F32)
    acted_grad = acted_grad + jnp.dot(earlier, full[2].T, preferred_element_type=F32)
    input_grad = (cot.astype(F32) + gelu_grad(rows.astype(F32), acted_grad)).astype(BF16)
    grads = reduce_grads(scale, acted, cot, later, hg, earlier, gated)
    return (
        outputs.reshape(batch, local_len, chans),
        input_grad.reshape(batch, local_len, chans),
        grads[:3].transpose(1, 0, 2),
        grads[3],
    )


def solution(mesh):
    fast = mesh.shape["seq"] == SEQ
    return jax.shard_map(
        pair_shards if fast else shards,
        mesh=mesh,
        in_specs=(
            P("groups", "seq", None),
            P(None, "seq", None),
            P("seq", None),
            P("groups", "seq", None),
        ),
        out_specs=(
            P("groups", "seq", None),
            P("groups", "seq", None),
            P(("groups", "seq"), None, None),
            P(("groups", "seq"), None),
        ),
        check_vma=False,
    )
```

```python
import functools

import jax
import jax.numpy as jnp
from jax import lax
from jax.experimental import pallas as pl
from jax.experimental.pallas import tpu as pltpu
from jax.sharding import PartitionSpec as P

L = 8192


def from_behind(block, axis, distance):
    devices = range(lax.axis_size(axis))
    route = [(i - distance, i) for i in devices if i - distance in devices]
    return lax.ppermute(block, axis, route)


def gelu_grad(point, upstream):
    return jax.vjp(jax.nn.gelu, point)[1](upstream)[0]


def shards(inputs, conv_weight, proj_weight, cotangent):
    batch, local_len, chans = inputs.shape
    devices = lax.axis_size("seq")
    stride = devices // 8
    scale = 1.0 / float(batch * L) ** 0.5
    acted = jax.nn.gelu(inputs.astype(jnp.float32)).astype(jnp.bfloat16)
    conv_weight, proj_weight = (
        lax.all_gather(conv_weight, "seq", axis=1, tiled=True),
        lax.all_gather(proj_weight, "seq", axis=0, tiled=True),
    )
    hid = conv_weight.shape[2]
    acted_rows = acted.reshape(-1, chans)
    before = from_behind(acted, "seq", stride)
    after = from_behind(acted, "seq", -stride)
    hidden = jnp.dot(before.reshape(-1, chans), conv_weight[0], preferred_element_type=jnp.float32)
    hidden = hidden + jnp.dot(acted_rows, conv_weight[1], preferred_element_type=jnp.float32)
    hidden = hidden + jnp.dot(
        after.reshape(-1, chans), conv_weight[2], preferred_element_type=jnp.float32
    )
    gated = jax.nn.gelu(hidden).astype(jnp.bfloat16)
    outputs = (
        inputs.reshape(-1, chans).astype(jnp.float32)
        + jnp.dot(gated, proj_weight.T, preferred_element_type=jnp.float32)
    ).astype(jnp.bfloat16)
    cot_rows = cotangent.reshape(-1, chans)
    gated_grad = jnp.dot(cot_rows, proj_weight, preferred_element_type=jnp.float32)
    hidden_grad = gelu_grad(hidden, gated_grad).astype(jnp.bfloat16)
    grad_blocks = hidden_grad.reshape(batch, local_len, hid)
    grad_later = from_behind(grad_blocks, "seq", -stride).reshape(-1, hid)
    grad_earlier = from_behind(grad_blocks, "seq", stride).reshape(-1, hid)
    acted_grad = jnp.dot(grad_later, conv_weight[0].T, preferred_element_type=jnp.float32)
    acted_grad = acted_grad + jnp.dot(
        hidden_grad, conv_weight[1].T, preferred_element_type=jnp.float32
    )
    acted_grad = acted_grad + jnp.dot(
        grad_earlier, conv_weight[2].T, preferred_element_type=jnp.float32
    )
    input_grad = (
        cot_rows.astype(jnp.float32)
        + gelu_grad(inputs.reshape(-1, chans).astype(jnp.float32), acted_grad)
    ).astype(jnp.bfloat16)
    tap_grads = (grad_later, hidden_grad, grad_earlier)
    share = chans // devices
    local_terms = [
        jnp.dot(acted_rows.T, piece, preferred_element_type=jnp.float32) for piece in tap_grads
    ]
    local_terms.append(jnp.dot(cot_rows.T, gated, preferred_element_type=jnp.float32))
    stacked = jnp.stack(local_terms, axis=1)
    received = lax.all_to_all(stacked, "seq", split_axis=0, concat_axis=0, tiled=True)
    summed = jnp.sum(received.reshape(devices, share, 4, received.shape[2]), axis=0)
    conv_sum = summed[:, 0:3, :]
    proj_sum = summed[:, 3, :]
    return (
        outputs.reshape(batch, local_len, chans),
        input_grad.reshape(batch, local_len, chans),
        conv_sum * scale,
        proj_sum * scale,
    )


F32 = jnp.float32
BF16 = jnp.bfloat16
MESH = pl.DeviceIdType.MESH
VMEM = pl.BlockSpec(memory_space=pltpu.VMEM)
HBM = pl.BlockSpec(memory_space=pl.ANY)
SEQ = 16
CHUNKS = 4
COEF = 0.7978845608028654
CUBE = 0.044715


def place():
    s = lax.axis_index("seq")
    return s // 4, (s // 2) % 2, s % 2


def index(z, x, core):
    return (z * 2 + x) * 2 + core


def copy_to(src, dst, send, recv, target):
    return pltpu.make_async_remote_copy(
        src_ref=src, dst_ref=dst, send_sem=send, recv_sem=recv,
        device_id={"seq": target}, device_id_type=MESH,
    )


def greet(targets):
    barrier = pltpu.get_barrier_semaphore()
    for target in targets:
        pl.semaphore_signal(barrier, inc=1, device_id={"seq": target}, device_id_type=MESH)
    pl.semaphore_wait(barrier, len(targets))


def gelu_parts(v):
    t = jnp.tanh(COEF * (v + CUBE * v * v * v))
    half = 0.5 * (1.0 + t)
    return half * v, half + (0.5 * COEF) * v * (1.0 - t * t) * (1.0 + (3.0 * CUBE) * v * v)


def params(cid, mib=56):
    return pltpu.CompilerParams(
        collective_id=cid, has_side_effects=True, vmem_limit_bytes=mib * 1024 * 1024
    )


def gather_kernel(w_ref, x_ref, full_ref, acted_ref, own_sem, zs, zr, xs, xr, cs, cr):
    z, x, core = place()
    share = w_ref.shape[1]
    zt = [lax.rem(z + d, 4) for d in range(4)]
    zf = [lax.rem(z + 4 - d, 4) for d in range(4)]

    def rows(zz, xx, cc):
        start = pl.multiple_of(index(zz, xx, cc) * share, share)
        return full_ref.at[:, pl.ds(start, share), :]

    greet([index(zt[d], x, core) for d in (1, 2, 3)]
          + [index(z, 1 - x, core), index(z, x, 1 - core)])
    mine = rows(z, x, core)
    copies = []
    for d in (1, 3, 2):
        copies.append(copy_to(w_ref, mine, zs.at[d], zr.at[d], index(zt[d], x, core)))
        copies[-1].start()
    zc = dict(zip((1, 3, 2), copies))

    def to_x(j, src):
        c = copy_to(src, rows(zf[j], x, core), xs.at[j], xr.at[j], index(z, 1 - x, core))
        c.start()
        return c

    def to_core(j, src, xx):
        c = copy_to(src, rows(zf[j % 4], xx, core), cs.at[j], cr.at[j], index(z, x, 1 - core))
        c.start()
        return c

    xc = {0: to_x(0, w_ref)}
    cc = {0: to_core(0, w_ref, x)}
    own = pltpu.make_async_copy(w_ref, mine, own_sem)
    own.start()

    tile = 64

    def act(i, carry):
        r = pl.ds(pl.multiple_of(i * tile, tile), tile)
        v = x_ref[r, :].astype(F32)
        t = jnp.tanh(COEF * (v + CUBE * v * v * v))
        acted_ref[r, :] = (0.5 * v * (1.0 + t)).astype(BF16)
        return carry

    lax.fori_loop(0, x_ref.shape[0] // tile, act, 0)

    def take_z(j):
        zc[j].wait_recv()
        src = rows(zf[j], x, core)
        xc[j] = to_x(j, src)
        cc[j] = to_core(j, src, x)

    def take_x(j):
        xc[j].wait_recv()
        cc[4 + j] = to_core(4 + j, rows(zf[j], 1 - x, core), 1 - x)

    take_z(1)
    take_z(3)
    take_x(0)
    take_z(2)
    take_x(1)
    take_x(3)
    take_x(2)
    for j in range(8):
        cc[j].wait_recv()
    own.wait()
    for j in (1, 2, 3):
        zc[j].wait_send()
    for j in range(4):
        xc[j].wait_send()
    for j in range(8):
        cc[j].wait_send()


def gather(w4, flat):
    taps, share, hid = w4.shape
    dma = pltpu.SemaphoreType.DMA
    return pl.pallas_call(
        gather_kernel,
        out_shape=(
            jax.ShapeDtypeStruct((taps, share * SEQ, hid), BF16),
            jax.ShapeDtypeStruct(flat.shape, BF16),
        ),
        in_specs=[HBM, VMEM],
        out_specs=(HBM, VMEM),
        scratch_shapes=[dma, dma((4,)), dma((4,)), dma((4,)), dma((4,)), dma((8,)), dma((8,))],
        compiler_params=params(0),
        name="gather_weights",
    )(w4, flat)


def forward_kernel(acted_ref, w_ref, cot_ref, gated_ref, hg_ref,
                   out_a, in_a, out_s, in_s, part, gg, zs, zr, xs, xr):
    z, x, core = place()
    up = x == 1
    sends = jnp.logical_or(jnp.logical_and(up, z < 3), jnp.logical_and(x == 0, z > 0))
    takes = jnp.logical_or(jnp.logical_and(up, z > 0), jnp.logical_and(x == 0, z < 3))
    step = 2 * x - 1
    ahead = index(lax.rem(z + step + 4, 4), x, core)
    behind = index(lax.rem(z - step + 4, 4), x, core)
    across = index(z, 1 - x, core)
    greet([ahead, behind, across])
    n = acted_ref.shape[0] // CHUNKS
    tap_far = 2 - 2 * x
    tap_near = 2 * x

    def rows(i):
        return pl.ds(pl.multiple_of(i * n, n), n)

    def z_copy(i):
        return copy_to(out_a.at[i], in_a.at[i], zs.at[i], zr.at[i], ahead)

    def x_copy(i):
        return copy_to(out_s.at[i], in_s.at[i], xs.at[i], xr.at[i], across)

    def far(i, carry):
        out_a[i] = jnp.dot(acted_ref[rows(i), :], w_ref[tap_far], preferred_element_type=F32).astype(BF16)

        @pl.when(sends)
        def _():
            z_copy(i).start()
        return carry

    lax.fori_loop(0, CHUNKS, far, 0)

    def near(i, carry):
        part[i] = jnp.dot(acted_ref[rows(i), :], w_ref[tap_near], preferred_element_type=F32)
        gg[i] = jnp.dot(cot_ref[rows(i), :], w_ref[3], preferred_element_type=F32)
        return carry

    lax.fori_loop(0, CHUNKS, near, 0)

    def combine(i, carry):
        @pl.when(takes)
        def _():
            z_copy(i).wait_recv()
            part[i] = part[i] + in_a[i].astype(F32)
        out_s[i] = part[i].astype(BF16)
        x_copy(i).start()
        part[i] = jnp.dot(acted_ref[rows(i), :], w_ref[1], preferred_element_type=F32)
        return carry

    lax.fori_loop(0, CHUNKS, combine, 0)

    def finish(i, carry):
        x_copy(i).wait_recv()
        hidden = part[i] + in_s[i].astype(F32)
        value, slope = gelu_parts(hidden)
        gated_ref[rows(i), :] = value.astype(BF16)
        hg_ref[rows(i), :] = (gg[i] * slope).astype(BF16)
        return carry

    lax.fori_loop(0, CHUNKS, finish, 0)

    def drain(i, carry):
        x_copy(i).wait_send()

        @pl.when(sends)
        def _():
            z_copy(i).wait_send()
        return carry

    lax.fori_loop(0, CHUNKS, drain, 0)


def forward(acted, w4, cot):
    m = acted.shape[0]
    hid = w4.shape[2]
    dma = pltpu.SemaphoreType.DMA
    block = (CHUNKS, m // CHUNKS, hid)
    return pl.pallas_call(
        forward_kernel,
        out_shape=(jax.ShapeDtypeStruct((m, hid), BF16),) * 2,
        in_specs=[VMEM] * 3,
        out_specs=(VMEM, VMEM),
        scratch_shapes=[pltpu.VMEM(block, BF16)] * 4 + [pltpu.VMEM(block, F32)] * 2
        + [dma((CHUNKS,))] * 4,
        compiler_params=params(1),
        name="forward_halo",
    )(acted, w4, cot)


ORDER = (2, 1, 3, 0)
PASSES = ((1, 3), (0, 2))
NT = (((1,), (1,)), ((), ()))
TN = (((0,), (0,)), ((), ()))


def backward_kernel(scale, hg_ref, acted_ref, cot_ref, gated_ref, x_hbm, w_hbm,
                    grads_ref, outputs_hbm, input_grad_hbm,
                    x_buf, w_buf, o_buf, g_buf, near, give, keep, got, acc,
                    x_out, x_in, z_out, z_in, load, store,
                    hzs, hzr, hxs, hxr, cs, cr, xs, xr, zs, zr, free):
    z, x, core = place()
    share = grads_ref.shape[1]
    zt = [lax.rem(z + d, 4) for d in range(4)]
    across = index(z, 1 - x, core)
    other = index(z, x, 1 - core)
    even = x == 0
    sends = jnp.logical_or(jnp.logical_and(even, z < 3), jnp.logical_and(x == 1, z > 0))
    takes = jnp.logical_or(jnp.logical_and(even, z > 0), jnp.logical_and(x == 1, z < 3))
    ahead = index(lax.rem(z + (1 - 2 * x) + 4, 4), x, core)
    w_load = pltpu.make_async_copy(w_hbm, w_buf, load.at[0])
    x_load = pltpu.make_async_copy(x_hbm, x_buf, load.at[1])
    w_load.start()
    x_load.start()
    greet([index(zt[d], x, core) for d in (1, 2, 3)] + [across, other])
    wide = 4 * share
    tile = 256
    m, hid = hg_ref.shape
    chans = acted_ref.shape[1]
    n = m // CHUNKS

    def rows(i):
        return pl.ds(pl.multiple_of(i * n, n), n)

    def halo_x(i):
        return copy_to(hg_ref.at[rows(i), :], near.at[0, rows(i), :], hxs.at[i], hxr.at[i], across)

    def halo_z(i):
        return copy_to(near.at[0, rows(i), :], near.at[1, rows(i), :], hzs.at[i], hzr.at[i], ahead)

    def core_copy(s):
        return copy_to(give.at[s % 2], got.at[s % 2], cs.at[s], cr.at[s], other)

    def x_copy(s):
        return copy_to(x_out.at[s], x_in.at[s], xs.at[s], xr.at[s], across)

    def z_copy(s):
        j = s // 4 * 3 + s % 4
        target = index(zt[ORDER[s % 4]], x, core)
        return copy_to(z_out.at[j], z_in.at[j], zs.at[j], zr.at[j], target)

    def onward(i):
        halo_x(i).wait_recv()

        @pl.when(sends)
        def _():
            halo_z(i).start()

    def compute(s):
        if s >= 2:
            core_copy(s - 2).wait_send()
        cols = pl.ds(pl.multiple_of(zt[ORDER[s % 4]] * wide, wide), wide)
        for j, k in enumerate(PASSES[s // 4]):
            left = cot_ref if k == 3 else acted_ref

            def part(i, carry, k=k, j=j, left=left):
                t = pl.ds(pl.multiple_of(i * tile, tile), tile)
                if k == 3:
                    right = gated_ref[:, t]
                elif k == 1:
                    right = hg_ref[:, t]
                else:
                    right = near[x if k == 0 else 1 - x, :, t]
                p = lax.dot_general(left[:, cols], right, TN, preferred_element_type=F32)
                for xx in range(2):
                    lo = p[2 * xx * share:(2 * xx + 1) * share]
                    hi = p[(2 * xx + 1) * share:(2 * xx + 2) * share]
                    keep[s % 2, xx, j, :, t] = jnp.where(core == 0, lo, hi)
                    give[s % 2, xx, j, :, t] = jnp.where(core == 0, hi, lo)
                return carry

            lax.fori_loop(0, hid // tile, part, 0)
        if s >= 2:
            pl.semaphore_wait(free, 1)
        core_copy(s).start()

    def to_across(s):
        core_copy(s).wait_recv()

        def add(j, carry):
            x_out[s, j] = (keep[s % 2, 1 - x, j] + got[s % 2, 1 - x, j]).astype(BF16)
            acc[s, j] = keep[s % 2, x, j] + got[s % 2, x, j]
            return carry

        lax.fori_loop(0, 2, add, 0)
        x_copy(s).start()
        if s < 6:
            pl.semaphore_signal(free, inc=1, device_id={"seq": other}, device_id_type=MESH)

    def to_z(s):
        x_copy(s).wait_recv()
        for j in range(2):
            z_out[s // 4 * 3 + s % 4, j] = (acc[s, j] + x_in[s, j].astype(F32)).astype(BF16)
        z_copy(s).start()

    span = 512

    def out_store(i):
        return pltpu.make_async_copy(o_buf.at[rows(i), :], outputs_hbm.at[rows(i), :], store.at[i])

    def grad_store(i):
        return pltpu.make_async_copy(
            g_buf.at[rows(i), :], input_grad_hbm.at[rows(i), :], store.at[CHUNKS + i]
        )

    def project(i, carry):
        def part(j, c):
            t = pl.ds(pl.multiple_of(j * span, span), span)
            p = lax.dot_general(gated_ref[rows(i), :], w_buf[3, t, :], NT, preferred_element_type=F32)
            o_buf[rows(i), t] = (x_buf[rows(i), t].astype(F32) + p).astype(BF16)
            return c

        lax.fori_loop(0, chans // span, part, 0)
        out_store(i).start()
        return carry

    def spread(i, carry):
        def part(j, c):
            t = pl.ds(pl.multiple_of(j * span, span), span)
            p = lax.dot_general(hg_ref[rows(i), :], w_buf[1, t, :], NT, preferred_element_type=F32)
            p += lax.dot_general(near[x, rows(i), :], w_buf[0, t, :], NT, preferred_element_type=F32)
            p += lax.dot_general(near[1 - x, rows(i), :], w_buf[2, t, :], NT, preferred_element_type=F32)
            slope = gelu_parts(x_buf[rows(i), t].astype(F32))[1]
            g_buf[rows(i), t] = (cot_ref[rows(i), t].astype(F32) + p * slope).astype(BF16)
            return c

        lax.fori_loop(0, chans // span, part, 0)
        grad_store(i).start()
        return carry

    for i in range(CHUNKS):
        halo_x(i).start()

    @pl.when(jnp.logical_not(takes))
    def _():
        near[1] = jnp.zeros((m, hid), BF16)

    compute(0)
    compute(1)
    onward(0)
    to_across(0)
    compute(2)
    onward(1)
    to_across(1)
    compute(3)
    onward(2)
    to_across(2)
    to_z(0)
    onward(3)
    to_across(3)
    w_load.wait()
    x_load.wait()
    lax.fori_loop(0, CHUNKS, project, 0)
    to_z(1)
    to_z(2)

    @pl.when(takes)
    def _():
        for i in range(CHUNKS):
            halo_z(i).wait_recv()

    compute(4)
    compute(5)
    to_across(4)
    compute(6)
    to_across(5)
    compute(7)
    to_across(6)
    to_z(4)
    to_across(7)
    lax.fori_loop(0, 2, spread, 0)
    to_z(5)
    lax.fori_loop(2, CHUNKS, spread, 0)
    to_z(6)
    for s in (3, 7):
        x_copy(s).wait_recv()
        for j in range(s // 4 * 3, s // 4 * 3 + 3):
            z_copy(s // 4 * 4 + j % 3).wait_recv()
        for j in range(2):
            own = acc[s, j] + x_in[s, j].astype(F32)
            for i in range(s // 4 * 3, s // 4 * 3 + 3):
                own = own + z_in[i, j].astype(F32)
            grads_ref[PASSES[s // 4][j]] = own * scale
    for i in range(CHUNKS):
        out_store(i).wait()
        grad_store(i).wait()
        halo_x(i).wait_send()

    @pl.when(sends)
    def _():
        for i in range(CHUNKS):
            halo_z(i).wait_send()

    core_copy(6).wait_send()
    core_copy(7).wait_send()
    for s in range(8):
        x_copy(s).wait_send()
        if s % 4 < 3:
            z_copy(s).wait_send()


def backward(scale, hg, acted, cot, gated, rows, full):
    m, hid = hg.shape
    chans = acted.shape[1]
    share = chans // SEQ
    dma = pltpu.SemaphoreType.DMA
    pair = (2, 2, share, hid)
    return pl.pallas_call(
        functools.partial(backward_kernel, scale),
        out_shape=(
            jax.ShapeDtypeStruct((4, share, hid), F32),
            jax.ShapeDtypeStruct((m, chans), BF16),
            jax.ShapeDtypeStruct((m, chans), BF16),
        ),
        in_specs=[VMEM] * 4 + [HBM] * 2,
        out_specs=(VMEM, HBM, HBM),
        scratch_shapes=[
            pltpu.VMEM((m, chans), BF16),
            pltpu.VMEM(full.shape, BF16),
            pltpu.VMEM((m, chans), BF16),
            pltpu.VMEM((m, chans), BF16),
            pltpu.VMEM((2, m, hid), BF16),
            pltpu.VMEM((2,) + pair, F32),
            pltpu.VMEM((2,) + pair, F32),
            pltpu.VMEM((2,) + pair, F32),
            pltpu.VMEM((8, 2, share, hid), F32),
            pltpu.VMEM((8, 2, share, hid), BF16),
            pltpu.VMEM((8, 2, share, hid), BF16),
            pltpu.VMEM((6, 2, share, hid), BF16),
            pltpu.VMEM((6, 2, share, hid), BF16),
            dma((2,)), dma((2 * CHUNKS,)),
            dma((CHUNKS,)), dma((CHUNKS,)), dma((CHUNKS,)), dma((CHUNKS,)),
            dma((8,)), dma((8,)), dma((8,)), dma((8,)), dma((6,)), dma((6,)),
            pltpu.SemaphoreType.REGULAR,
        ],
        compiler_params=params(2, 62),
        name="backward_halo_and_reduce",
    )(hg, acted, cot, gated, rows, full)


def pair_shards(inputs, conv_weight, proj_weight, cotangent):
    batch, local_len, chans = inputs.shape
    scale = 1.0 / float(batch * L) ** 0.5
    rows = inputs.reshape(-1, chans)
    cot = cotangent.reshape(-1, chans)
    full, acted = gather(jnp.concatenate([conv_weight, proj_weight[None]], axis=0), rows)
    gated, hg = forward(acted, full, cot)
    grads, outputs, input_grad = backward(scale, hg, acted, cot, gated, rows, full)
    return (
        outputs.reshape(batch, local_len, chans),
        input_grad.reshape(batch, local_len, chans),
        grads[:3].transpose(1, 0, 2),
        grads[3],
    )


def solution(mesh):
    fast = mesh.shape["seq"] == SEQ
    return jax.shard_map(
        pair_shards if fast else shards,
        mesh=mesh,
        in_specs=(
            P("groups", "seq", None),
            P(None, "seq", None),
            P("seq", None),
            P("groups", "seq", None),
        ),
        out_specs=(
            P("groups", "seq", None),
            P("groups", "seq", None),
            P(("groups", "seq"), None, None),
            P(("groups", "seq"), None),
        ),
        check_vma=False,
    )
```

```python
import functools

import jax
import jax.numpy as jnp
from jax import lax
from jax.experimental import pallas as pl
from jax.experimental.pallas import tpu as pltpu
from jax.sharding import PartitionSpec as P

L = 8192


def from_behind(block, axis, distance):
    devices = range(lax.axis_size(axis))
    route = [(i - distance, i) for i in devices if i - distance in devices]
    return lax.ppermute(block, axis, route)


def gelu_grad(point, upstream):
    return jax.vjp(jax.nn.gelu, point)[1](upstream)[0]


def shards(inputs, conv_weight, proj_weight, cotangent):
    batch, local_len, chans = inputs.shape
    devices = lax.axis_size("seq")
    stride = devices // 8
    scale = 1.0 / float(batch * L) ** 0.5
    acted = jax.nn.gelu(inputs.astype(jnp.float32)).astype(jnp.bfloat16)
    conv_weight, proj_weight = (
        lax.all_gather(conv_weight, "seq", axis=1, tiled=True),
        lax.all_gather(proj_weight, "seq", axis=0, tiled=True),
    )
    hid = conv_weight.shape[2]
    acted_rows = acted.reshape(-1, chans)
    before = from_behind(acted, "seq", stride)
    after = from_behind(acted, "seq", -stride)
    hidden = jnp.dot(before.reshape(-1, chans), conv_weight[0], preferred_element_type=jnp.float32)
    hidden = hidden + jnp.dot(acted_rows, conv_weight[1], preferred_element_type=jnp.float32)
    hidden = hidden + jnp.dot(
        after.reshape(-1, chans), conv_weight[2], preferred_element_type=jnp.float32
    )
    gated = jax.nn.gelu(hidden).astype(jnp.bfloat16)
    outputs = (
        inputs.reshape(-1, chans).astype(jnp.float32)
        + jnp.dot(gated, proj_weight.T, preferred_element_type=jnp.float32)
    ).astype(jnp.bfloat16)
    cot_rows = cotangent.reshape(-1, chans)
    gated_grad = jnp.dot(cot_rows, proj_weight, preferred_element_type=jnp.float32)
    hidden_grad = gelu_grad(hidden, gated_grad).astype(jnp.bfloat16)
    grad_blocks = hidden_grad.reshape(batch, local_len, hid)
    grad_later = from_behind(grad_blocks, "seq", -stride).reshape(-1, hid)
    grad_earlier = from_behind(grad_blocks, "seq", stride).reshape(-1, hid)
    acted_grad = jnp.dot(grad_later, conv_weight[0].T, preferred_element_type=jnp.float32)
    acted_grad = acted_grad + jnp.dot(
        hidden_grad, conv_weight[1].T, preferred_element_type=jnp.float32
    )
    acted_grad = acted_grad + jnp.dot(
        grad_earlier, conv_weight[2].T, preferred_element_type=jnp.float32
    )
    input_grad = (
        cot_rows.astype(jnp.float32)
        + gelu_grad(inputs.reshape(-1, chans).astype(jnp.float32), acted_grad)
    ).astype(jnp.bfloat16)
    tap_grads = (grad_later, hidden_grad, grad_earlier)
    share = chans // devices
    local_terms = [
        jnp.dot(acted_rows.T, piece, preferred_element_type=jnp.float32) for piece in tap_grads
    ]
    local_terms.append(jnp.dot(cot_rows.T, gated, preferred_element_type=jnp.float32))
    stacked = jnp.stack(local_terms, axis=1)
    received = lax.all_to_all(stacked, "seq", split_axis=0, concat_axis=0, tiled=True)
    summed = jnp.sum(received.reshape(devices, share, 4, received.shape[2]), axis=0)
    conv_sum = summed[:, 0:3, :]
    proj_sum = summed[:, 3, :]
    return (
        outputs.reshape(batch, local_len, chans),
        input_grad.reshape(batch, local_len, chans),
        conv_sum * scale,
        proj_sum * scale,
    )


F32 = jnp.float32
BF16 = jnp.bfloat16
MESH = pl.DeviceIdType.MESH
VMEM = pl.BlockSpec(memory_space=pltpu.VMEM)
HBM = pl.BlockSpec(memory_space=pl.ANY)
SEQ = 16
CHUNKS = 4
COEF = 0.7978845608028654
CUBE = 0.044715


def place():
    s = lax.axis_index("seq")
    return s // 4, (s // 2) % 2, s % 2


def index(z, x, core):
    return (z * 2 + x) * 2 + core


def copy_to(src, dst, send, recv, target):
    return pltpu.make_async_remote_copy(
        src_ref=src, dst_ref=dst, send_sem=send, recv_sem=recv,
        device_id={"seq": target}, device_id_type=MESH,
    )


def greet(targets):
    barrier = pltpu.get_barrier_semaphore()
    for target in targets:
        pl.semaphore_signal(barrier, inc=1, device_id={"seq": target}, device_id_type=MESH)
    pl.semaphore_wait(barrier, len(targets))


def gelu_parts(v):
    t = jnp.tanh(COEF * (v + CUBE * v * v * v))
    half = 0.5 * (1.0 + t)
    return half * v, half + (0.5 * COEF) * v * (1.0 - t * t) * (1.0 + (3.0 * CUBE) * v * v)


def params(cid, mib=56):
    return pltpu.CompilerParams(
        collective_id=cid, has_side_effects=True, vmem_limit_bytes=mib * 1024 * 1024
    )


def forward_kernel(w_ref, x_ref, cot_ref, full_hbm, acted_ref, gated_ref, hg_ref,
                   w_buf, out_a, in_a, out_s, in_s, part, gg, own_sem,
                   zs0, zr0, xs0, xr0, cs0, cr0, zs1, zr1, xs1, xr1, cs1, cr1,
                   ys, yr, fs, fr, hzs, hzr, hxs, hxr):
    z, x, core = place()
    group = lax.axis_index("groups")
    me = lax.axis_index("seq")
    share = w_ref.shape[1]
    zt = [lax.rem(z + d, 4) for d in range(4)]
    zf = [lax.rem(z + 4 - d, 4) for d in range(4)]
    across = index(z, 1 - x, core)
    other = index(z, x, 1 - core)
    up = x == 1
    sends = jnp.logical_or(jnp.logical_and(up, z < 3), jnp.logical_and(x == 0, z > 0))
    takes = jnp.logical_or(jnp.logical_and(up, z > 0), jnp.logical_and(x == 0, z < 3))
    ahead = index(lax.rem(z + (2 * x - 1) + 4, 4), x, core)

    barrier = pltpu.get_barrier_semaphore()
    for target in [index(zt[d], x, core) for d in (1, 2, 3)] + [across, other]:
        pl.semaphore_signal(barrier, inc=1, device_id={"seq": target}, device_id_type=MESH)
    pl.semaphore_signal(
        barrier, inc=1, device_id={"groups": 1 - group, "seq": me}, device_id_type=MESH
    )
    pl.semaphore_wait(barrier, 6)

    def slab(first, count, zz, xx):
        start = pl.multiple_of(index(zz, xx, core) * share, share)
        return w_buf.at[pl.ds(first, count), pl.ds(start, share), :]

    own_tap = 2 + group
    far_tap = 3 - group
    passes = ((0, 2, zs0, zr0, xs0, xr0, cs0, cr0), (own_tap, 1, zs1, zr1, xs1, xr1, cs1, cr1))

    def column(j):
        return zf[j % 4], (x if j < 4 else 1 - x)

    def z_copy(p, d):
        first, count, send, recv = passes[p][:4]
        return copy_to(w_ref.at[pl.ds(first, count)], slab(first, count, z, x),
                       send.at[d], recv.at[d], index(zt[d], x, core))

    def x_copy(p, j):
        first, count, _, _, send, recv = passes[p][:6]
        place_ = slab(first, count, zf[j], x)
        return copy_to(w_ref.at[pl.ds(first, count)] if j == 0 else place_, place_,
                       send.at[j], recv.at[j], across)

    def core_copy(p, j):
        first, count, _, _, _, _, send, recv = passes[p]
        if j == 0:
            return copy_to(w_ref.at[pl.ds(2 * p, 2)], slab(2 * p, 2, z, x),
                           send.at[0], recv.at[0], other)
        place_ = slab(first, count, *column(j))
        return copy_to(place_, place_, send.at[j], recv.at[j], other)

    def y_copy(j):
        place_ = slab(own_tap, 1, *column(j))
        return pltpu.make_async_remote_copy(
            src_ref=place_, dst_ref=place_, send_sem=ys.at[j], recv_sem=yr.at[j],
            device_id={"groups": 1 - group, "seq": me}, device_id_type=MESH,
        )

    def relay_copy(j):
        place_ = slab(far_tap, 1, *column(j))
        return copy_to(place_, place_, fs.at[j], fr.at[j], other)

    def begin(p):
        for d in (1, 3, 2):
            z_copy(p, d).start()
        x_copy(p, 0).start()
        core_copy(p, 0).start()

    def take_z(p, j):
        z_copy(p, j).wait_recv()
        x_copy(p, j).start()
        core_copy(p, j).start()
        if p == 1:
            y_copy(j).start()

    def take_x(p, j):
        x_copy(p, j).wait_recv()
        core_copy(p, 4 + j).start()
        if p == 1:
            y_copy(4 + j).start()

    n = acted_ref.shape[0] // CHUNKS

    def rows(i):
        return pl.ds(pl.multiple_of(i * n, n), n)

    def halo_z(i):
        return copy_to(out_a.at[i], in_a.at[i], hzs.at[i], hzr.at[i], ahead)

    def halo_x(i):
        return copy_to(out_s.at[i], in_s.at[i], hxs.at[i], hxr.at[i], across)

    begin(0)
    own = pltpu.make_async_copy(w_ref, slab(0, 4, z, x), own_sem.at[0])
    own.start()
    tile = 64

    def act(i, carry):
        r = pl.ds(pl.multiple_of(i * tile, tile), tile)
        v = x_ref[r, :].astype(F32)
        t = jnp.tanh(COEF * (v + CUBE * v * v * v))
        acted_ref[r, :] = (0.5 * v * (1.0 + t)).astype(BF16)
        return carry

    lax.fori_loop(0, x_ref.shape[0] // tile, act, 0)
    take_z(0, 1)
    take_z(0, 3)
    take_x(0, 0)
    take_z(0, 2)
    begin(1)
    take_x(0, 1)
    take_x(0, 3)
    take_x(0, 2)
    own.wait()
    for j in range(8):
        core_copy(0, j).wait_recv()

    def far(i, carry):
        out_a[i] = jnp.dot(acted_ref[rows(i), :], w_buf[1 - x], preferred_element_type=F32).astype(BF16)

        @pl.when(sends)
        def _():
            halo_z(i).start()
        return carry

    lax.fori_loop(0, CHUNKS, far, 0)
    take_z(1, 1)
    take_z(1, 3)
    take_x(1, 0)

    def near(i, carry):
        part[i] = jnp.dot(acted_ref[rows(i), :], w_buf[x], preferred_element_type=F32)
        return carry

    lax.fori_loop(0, CHUNKS, near, 0)
    take_z(1, 2)

    def combine(i):
        @pl.when(takes)
        def _():
            halo_z(i).wait_recv()
            part[i] = part[i] + in_a[i].astype(F32)
        out_s[i] = part[i].astype(BF16)
        halo_x(i).start()

    combine(0)
    take_x(1, 1)
    take_x(1, 3)
    combine(1)
    take_x(1, 2)
    combine(2)
    for j in (1, 3, 4, 2, 5, 7, 6):
        y_copy(j).wait_recv()
        relay_copy(j).start()
    combine(3)
    for j in range(8):
        core_copy(1, j).wait_recv()
    for j in range(1, 8):
        relay_copy(j).wait_recv()
    keep = pltpu.make_async_copy(w_buf, full_hbm, own_sem.at[1])
    keep.start()

    def middle(i, carry):
        part[i] = jnp.dot(acted_ref[rows(i), :], w_buf[2], preferred_element_type=F32)
        gg[i] = jnp.dot(cot_ref[rows(i), :], w_buf[3], preferred_element_type=F32)
        return carry

    lax.fori_loop(0, CHUNKS, middle, 0)

    def finish(i, carry):
        halo_x(i).wait_recv()
        hidden = part[i] + in_s[i].astype(F32)
        value, slope = gelu_parts(hidden)
        gated_ref[rows(i), :] = value.astype(BF16)
        hg_ref[rows(i), :] = (gg[i] * slope).astype(BF16)
        return carry

    lax.fori_loop(0, CHUNKS, finish, 0)
    for p in range(2):
        for d in (1, 2, 3):
            z_copy(p, d).wait_send()
        for j in range(4):
            x_copy(p, j).wait_send()
        for j in range(8):
            core_copy(p, j).wait_send()
    for j in range(1, 8):
        y_copy(j).wait_send()
        relay_copy(j).wait_send()
    for i in range(CHUNKS):
        halo_x(i).wait_send()

    @pl.when(sends)
    def _():
        for i in range(CHUNKS):
            halo_z(i).wait_send()

    keep.wait()


def forward(w4, flat, cot):
    taps, share, hid = w4.shape
    m = flat.shape[0]
    dma = pltpu.SemaphoreType.DMA
    block = (CHUNKS, m // CHUNKS, hid)
    full = jax.ShapeDtypeStruct((taps, share * SEQ, hid), BF16)
    return pl.pallas_call(
        forward_kernel,
        out_shape=(full, jax.ShapeDtypeStruct(flat.shape, BF16))
        + (jax.ShapeDtypeStruct((m, hid), BF16),) * 2,
        in_specs=[VMEM] * 3,
        out_specs=(HBM, VMEM, VMEM, VMEM),
        scratch_shapes=[pltpu.VMEM(full.shape, BF16)]
        + [pltpu.VMEM(block, BF16)] * 4 + [pltpu.VMEM(block, F32)] * 2
        + [dma((2,))] + ([dma((4,))] * 4 + [dma((8,))] * 2) * 2
        + [dma((8,))] * 4 + [dma((CHUNKS,))] * 4,
        compiler_params=params(1),
        name="gather_and_forward_halo",
    )(w4, flat, cot)


ORDER = (2, 1, 3, 0)
PASSES = ((1, 3), (0, 2))
NT = (((1,), (1,)), ((), ()))
TN = (((0,), (0,)), ((), ()))


def backward_kernel(scale, hg_ref, acted_ref, cot_ref, gated_ref, x_hbm, w_hbm,
                    grads_ref, outputs_hbm, input_grad_hbm,
                    x_buf, w_buf, o_buf, g_buf, near, give, keep, got, acc,
                    x_out, x_in, z_out, z_in, load, store,
                    hzs, hzr, hxs, hxr, cs, cr, xs, xr, zs, zr, free):
    z, x, core = place()
    share = grads_ref.shape[1]
    zt = [lax.rem(z + d, 4) for d in range(4)]
    across = index(z, 1 - x, core)
    other = index(z, x, 1 - core)
    even = x == 0
    sends = jnp.logical_or(jnp.logical_and(even, z < 3), jnp.logical_and(x == 1, z > 0))
    takes = jnp.logical_or(jnp.logical_and(even, z > 0), jnp.logical_and(x == 1, z < 3))
    ahead = index(lax.rem(z + (1 - 2 * x) + 4, 4), x, core)
    w_load = pltpu.make_async_copy(w_hbm, w_buf, load.at[0])
    x_load = pltpu.make_async_copy(x_hbm, x_buf, load.at[1])
    w_load.start()
    x_load.start()
    greet([index(zt[d], x, core) for d in (1, 2, 3)] + [across, other])
    wide = 4 * share
    tile = 256
    m, hid = hg_ref.shape
    chans = acted_ref.shape[1]
    n = m // CHUNKS

    def rows(i):
        return pl.ds(pl.multiple_of(i * n, n), n)

    def halo_x(i):
        return copy_to(hg_ref.at[rows(i), :], near.at[0, rows(i), :], hxs.at[i], hxr.at[i], across)

    def halo_z(i):
        return copy_to(near.at[0, rows(i), :], near.at[1, rows(i), :], hzs.at[i], hzr.at[i], ahead)

    def core_copy(s):
        return copy_to(give.at[s % 2], got.at[s % 2], cs.at[s], cr.at[s], other)

    def x_copy(s):
        return copy_to(x_out.at[s], x_in.at[s], xs.at[s], xr.at[s], across)

    def z_copy(s):
        j = s // 4 * 3 + s % 4
        target = index(zt[ORDER[s % 4]], x, core)
        return copy_to(z_out.at[j], z_in.at[j], zs.at[j], zr.at[j], target)

    def onward(i):
        halo_x(i).wait_recv()

        @pl.when(sends)
        def _():
            halo_z(i).start()

    def compute(s):
        if s >= 2:
            core_copy(s - 2).wait_send()
        cols = pl.ds(pl.multiple_of(zt[ORDER[s % 4]] * wide, wide), wide)
        for j, k in enumerate(PASSES[s // 4]):
            left = cot_ref if k == 3 else acted_ref

            def part(i, carry, k=k, j=j, left=left):
                t = pl.ds(pl.multiple_of(i * tile, tile), tile)
                if k == 3:
                    right = gated_ref[:, t]
                elif k == 1:
                    right = hg_ref[:, t]
                else:
                    right = near[x if k == 0 else 1 - x, :, t]
                p = lax.dot_general(left[:, cols], right, TN, preferred_element_type=F32)
                for xx in range(2):
                    lo = p[2 * xx * share:(2 * xx + 1) * share]
                    hi = p[(2 * xx + 1) * share:(2 * xx + 2) * share]
                    keep[s % 2, xx, j, :, t] = jnp.where(core == 0, lo, hi)
                    give[s % 2, xx, j, :, t] = jnp.where(core == 0, hi, lo)
                return carry

            lax.fori_loop(0, hid // tile, part, 0)
        if s >= 2:
            pl.semaphore_wait(free, 1)
        core_copy(s).start()

    def to_across(s):
        core_copy(s).wait_recv()

        def add(j, carry):
            x_out[s, j] = (keep[s % 2, 1 - x, j] + got[s % 2, 1 - x, j]).astype(BF16)
            acc[s, j] = keep[s % 2, x, j] + got[s % 2, x, j]
            return carry

        lax.fori_loop(0, 2, add, 0)
        x_copy(s).start()
        if s < 6:
            pl.semaphore_signal(free, inc=1, device_id={"seq": other}, device_id_type=MESH)

    def to_z(s):
        x_copy(s).wait_recv()
        for j in range(2):
            z_out[s // 4 * 3 + s % 4, j] = (acc[s, j] + x_in[s, j].astype(F32)).astype(BF16)
        z_copy(s).start()

    span = 512

    def out_store(i):
        return pltpu.make_async_copy(o_buf.at[rows(i), :], outputs_hbm.at[rows(i), :], store.at[i])

    def grad_store(i):
        return pltpu.make_async_copy(
            g_buf.at[rows(i), :], input_grad_hbm.at[rows(i), :], store.at[CHUNKS + i]
        )

    def project(i, carry):
        def part(j, c):
            t = pl.ds(pl.multiple_of(j * span, span), span)
            p = lax.dot_general(gated_ref[rows(i), :], w_buf[3, t, :], NT, preferred_element_type=F32)
            o_buf[rows(i), t] = (x_buf[rows(i), t].astype(F32) + p).astype(BF16)
            return c

        lax.fori_loop(0, chans // span, part, 0)
        out_store(i).start()
        return carry

    def spread(i, carry):
        def part(j, c):
            t = pl.ds(pl.multiple_of(j * span, span), span)
            p = lax.dot_general(hg_ref[rows(i), :], w_buf[2, t, :], NT, preferred_element_type=F32)
            p += lax.dot_general(near[x, rows(i), :], w_buf[0, t, :], NT, preferred_element_type=F32)
            p += lax.dot_general(near[1 - x, rows(i), :], w_buf[1, t, :], NT, preferred_element_type=F32)
            slope = gelu_parts(x_buf[rows(i), t].astype(F32))[1]
            g_buf[rows(i), t] = (cot_ref[rows(i), t].astype(F32) + p * slope).astype(BF16)
            return c

        lax.fori_loop(0, chans // span, part, 0)
        grad_store(i).start()
        return carry

    for i in range(CHUNKS):
        halo_x(i).start()

    @pl.when(jnp.logical_not(takes))
    def _():
        near[1] = jnp.zeros((m, hid), BF16)

    compute(0)
    compute(1)
    onward(0)
    to_across(0)
    compute(2)
    onward(1)
    to_across(1)
    compute(3)
    onward(2)
    to_across(2)
    to_z(0)
    onward(3)
    to_across(3)
    w_load.wait()
    x_load.wait()
    lax.fori_loop(0, CHUNKS, project, 0)
    to_z(1)
    to_z(2)

    @pl.when(takes)
    def _():
        for i in range(CHUNKS):
            halo_z(i).wait_recv()

    compute(4)
    compute(5)
    to_across(4)
    compute(6)
    to_across(5)
    compute(7)
    to_across(6)
    to_z(4)
    to_across(7)
    lax.fori_loop(0, 2, spread, 0)
    to_z(5)
    lax.fori_loop(2, CHUNKS, spread, 0)
    to_z(6)
    for s in (3, 7):
        x_copy(s).wait_recv()
        for j in range(s // 4 * 3, s // 4 * 3 + 3):
            z_copy(s // 4 * 4 + j % 3).wait_recv()
        for j in range(2):
            own = acc[s, j] + x_in[s, j].astype(F32)
            for i in range(s // 4 * 3, s // 4 * 3 + 3):
                own = own + z_in[i, j].astype(F32)
            grads_ref[PASSES[s // 4][j]] = own * scale
    for i in range(CHUNKS):
        out_store(i).wait()
        grad_store(i).wait()
        halo_x(i).wait_send()

    @pl.when(sends)
    def _():
        for i in range(CHUNKS):
            halo_z(i).wait_send()

    core_copy(6).wait_send()
    core_copy(7).wait_send()
    for s in range(8):
        x_copy(s).wait_send()
        if s % 4 < 3:
            z_copy(s).wait_send()


def backward(scale, hg, acted, cot, gated, rows, full):
    m, hid = hg.shape
    chans = acted.shape[1]
    share = chans // SEQ
    dma = pltpu.SemaphoreType.DMA
    pair = (2, 2, share, hid)
    return pl.pallas_call(
        functools.partial(backward_kernel, scale),
        out_shape=(
            jax.ShapeDtypeStruct((4, share, hid), F32),
            jax.ShapeDtypeStruct((m, chans), BF16),
            jax.ShapeDtypeStruct((m, chans), BF16),
        ),
        in_specs=[VMEM] * 4 + [HBM] * 2,
        out_specs=(VMEM, HBM, HBM),
        scratch_shapes=[
            pltpu.VMEM((m, chans), BF16),
            pltpu.VMEM(full.shape, BF16),
            pltpu.VMEM((m, chans), BF16),
            pltpu.VMEM((m, chans), BF16),
            pltpu.VMEM((2, m, hid), BF16),
            pltpu.VMEM((2,) + pair, F32),
            pltpu.VMEM((2,) + pair, F32),
            pltpu.VMEM((2,) + pair, F32),
            pltpu.VMEM((8, 2, share, hid), F32),
            pltpu.VMEM((8, 2, share, hid), BF16),
            pltpu.VMEM((8, 2, share, hid), BF16),
            pltpu.VMEM((6, 2, share, hid), BF16),
            pltpu.VMEM((6, 2, share, hid), BF16),
            dma((2,)), dma((2 * CHUNKS,)),
            dma((CHUNKS,)), dma((CHUNKS,)), dma((CHUNKS,)), dma((CHUNKS,)),
            dma((8,)), dma((8,)), dma((8,)), dma((8,)), dma((6,)), dma((6,)),
            pltpu.SemaphoreType.REGULAR,
        ],
        compiler_params=params(2, 62),
        name="backward_halo_and_reduce",
    )(hg, acted, cot, gated, rows, full)


def pair_shards(inputs, conv_weight, proj_weight, cotangent):
    batch, local_len, chans = inputs.shape
    scale = 1.0 / float(batch * L) ** 0.5
    rows = inputs.reshape(-1, chans)
    cot = cotangent.reshape(-1, chans)
    w4 = jnp.stack([conv_weight[0], conv_weight[2], conv_weight[1], proj_weight])
    full, acted, gated, hg = forward(w4, rows, cot)
    grads, outputs, input_grad = backward(scale, hg, acted, cot, gated, rows, full)
    return (
        outputs.reshape(batch, local_len, chans),
        input_grad.reshape(batch, local_len, chans),
        grads[:3].transpose(1, 0, 2),
        grads[3],
    )


def solution(mesh):
    fast = mesh.shape["seq"] == SEQ
    return jax.shard_map(
        pair_shards if fast else shards,
        mesh=mesh,
        in_specs=(
            P("groups", "seq", None),
            P(None, "seq", None),
            P("seq", None),
            P("groups", "seq", None),
        ),
        out_specs=(
            P("groups", "seq", None),
            P("groups", "seq", None),
            P(("groups", "seq"), None, None),
            P(("groups", "seq"), None),
        ),
        check_vma=False,
    )
```

```python
import functools

import jax
import jax.numpy as jnp
from jax import lax
from jax.experimental import pallas as pl
from jax.experimental.pallas import tpu as pltpu
from jax.sharding import PartitionSpec as P

L = 8192


def from_behind(block, axis, distance):
    devices = range(lax.axis_size(axis))
    route = [(i - distance, i) for i in devices if i - distance in devices]
    return lax.ppermute(block, axis, route)


def gelu_grad(point, upstream):
    return jax.vjp(jax.nn.gelu, point)[1](upstream)[0]


def shards(inputs, conv_weight, proj_weight, cotangent):
    batch, local_len, chans = inputs.shape
    devices = lax.axis_size("seq")
    stride = devices // 8
    scale = 1.0 / float(batch * L) ** 0.5
    acted = jax.nn.gelu(inputs.astype(jnp.float32)).astype(jnp.bfloat16)
    conv_weight, proj_weight = (
        lax.all_gather(conv_weight, "seq", axis=1, tiled=True),
        lax.all_gather(proj_weight, "seq", axis=0, tiled=True),
    )
    hid = conv_weight.shape[2]
    acted_rows = acted.reshape(-1, chans)
    before = from_behind(acted, "seq", stride)
    after = from_behind(acted, "seq", -stride)
    hidden = jnp.dot(before.reshape(-1, chans), conv_weight[0], preferred_element_type=jnp.float32)
    hidden = hidden + jnp.dot(acted_rows, conv_weight[1], preferred_element_type=jnp.float32)
    hidden = hidden + jnp.dot(
        after.reshape(-1, chans), conv_weight[2], preferred_element_type=jnp.float32
    )
    gated = jax.nn.gelu(hidden).astype(jnp.bfloat16)
    outputs = (
        inputs.reshape(-1, chans).astype(jnp.float32)
        + jnp.dot(gated, proj_weight.T, preferred_element_type=jnp.float32)
    ).astype(jnp.bfloat16)
    cot_rows = cotangent.reshape(-1, chans)
    gated_grad = jnp.dot(cot_rows, proj_weight, preferred_element_type=jnp.float32)
    hidden_grad = gelu_grad(hidden, gated_grad).astype(jnp.bfloat16)
    grad_blocks = hidden_grad.reshape(batch, local_len, hid)
    grad_later = from_behind(grad_blocks, "seq", -stride).reshape(-1, hid)
    grad_earlier = from_behind(grad_blocks, "seq", stride).reshape(-1, hid)
    acted_grad = jnp.dot(grad_later, conv_weight[0].T, preferred_element_type=jnp.float32)
    acted_grad = acted_grad + jnp.dot(
        hidden_grad, conv_weight[1].T, preferred_element_type=jnp.float32
    )
    acted_grad = acted_grad + jnp.dot(
        grad_earlier, conv_weight[2].T, preferred_element_type=jnp.float32
    )
    input_grad = (
        cot_rows.astype(jnp.float32)
        + gelu_grad(inputs.reshape(-1, chans).astype(jnp.float32), acted_grad)
    ).astype(jnp.bfloat16)
    tap_grads = (grad_later, hidden_grad, grad_earlier)
    share = chans // devices
    local_terms = [
        jnp.dot(acted_rows.T, piece, preferred_element_type=jnp.float32) for piece in tap_grads
    ]
    local_terms.append(jnp.dot(cot_rows.T, gated, preferred_element_type=jnp.float32))
    stacked = jnp.stack(local_terms, axis=1)
    received = lax.all_to_all(stacked, "seq", split_axis=0, concat_axis=0, tiled=True)
    summed = jnp.sum(received.reshape(devices, share, 4, received.shape[2]), axis=0)
    conv_sum = summed[:, 0:3, :]
    proj_sum = summed[:, 3, :]
    return (
        outputs.reshape(batch, local_len, chans),
        input_grad.reshape(batch, local_len, chans),
        conv_sum * scale,
        proj_sum * scale,
    )


F32 = jnp.float32
BF16 = jnp.bfloat16
MESH = pl.DeviceIdType.MESH
VMEM = pl.BlockSpec(memory_space=pltpu.VMEM)
HBM = pl.BlockSpec(memory_space=pl.ANY)
SEQ = 16
CHUNKS = 4
HALO = 8
COEF = 0.7978845608028654
CUBE = 0.044715


def place():
    s = lax.axis_index("seq")
    return s // 4, (s // 2) % 2, s % 2


def index(z, x, core):
    return (z * 2 + x) * 2 + core


def copy_to(src, dst, send, recv, target):
    return pltpu.make_async_remote_copy(
        src_ref=src, dst_ref=dst, send_sem=send, recv_sem=recv,
        device_id={"seq": target}, device_id_type=MESH,
    )


def greet(targets):
    barrier = pltpu.get_barrier_semaphore()
    for target in targets:
        pl.semaphore_signal(barrier, inc=1, device_id={"seq": target}, device_id_type=MESH)
    pl.semaphore_wait(barrier, len(targets))


def gelu_parts(v):
    t = jnp.tanh(COEF * (v + CUBE * v * v * v))
    half = 0.5 * (1.0 + t)
    return half * v, half + (0.5 * COEF) * v * (1.0 - t * t) * (1.0 + (3.0 * CUBE) * v * v)


def params(cid, mib=56):
    return pltpu.CompilerParams(
        collective_id=cid, has_side_effects=True, vmem_limit_bytes=mib * 1024 * 1024
    )


def forward_kernel(conv_hbm, proj_hbm, x_hbm, cot_hbm, full_hbm, acted_hbm, gated_ref, hg_ref,
                   w_buf, x_ref, cot_ref, acted_ref, out_a, in_a, out_s, in_s, part, gg, own_sem,
                   zs0, zr0, xs0, xr0, cs0, cr0, zs1, zr1, xs1, xr1, cs1, cr1,
                   ys, yr, fs, fr, hzs, hzr, hxs, hxr):
    z, x, core = place()
    group = lax.axis_index("groups")
    me = lax.axis_index("seq")
    share = proj_hbm.shape[0]
    zt = [lax.rem(z + d, 4) for d in range(4)]
    zf = [lax.rem(z + 4 - d, 4) for d in range(4)]
    across = index(z, 1 - x, core)
    other = index(z, x, 1 - core)
    up = x == 1
    sends = jnp.logical_or(jnp.logical_and(up, z < 3), jnp.logical_and(x == 0, z > 0))
    takes = jnp.logical_or(jnp.logical_and(up, z > 0), jnp.logical_and(x == 0, z < 3))
    ahead = index(lax.rem(z + (2 * x - 1) + 4, 4), x, core)

    mine = pl.ds(pl.multiple_of(me * share, share), share)
    loads = [
        pltpu.make_async_copy(conv_hbm.at[tap], w_buf.at[slot, mine, :], own_sem.at[slot])
        for slot, tap in enumerate((0, 2, 1))
    ]
    loads.append(pltpu.make_async_copy(proj_hbm, w_buf.at[3, mine, :], own_sem.at[3]))
    x_load = pltpu.make_async_copy(x_hbm, x_ref, own_sem.at[4])
    cot_load = pltpu.make_async_copy(cot_hbm, cot_ref, own_sem.at[5])
    for load in loads:
        load.start()
    x_load.start()
    cot_load.start()
    barrier = pltpu.get_barrier_semaphore()
    for target in [index(zt[d], x, core) for d in (1, 2, 3)] + [across, other]:
        pl.semaphore_signal(barrier, inc=1, device_id={"seq": target}, device_id_type=MESH)
    pl.semaphore_signal(
        barrier, inc=1, device_id={"groups": 1 - group, "seq": me}, device_id_type=MESH
    )
    pl.semaphore_wait(barrier, 6)

    def slab(first, count, zz, xx):
        start = pl.multiple_of(index(zz, xx, core) * share, share)
        return w_buf.at[pl.ds(first, count), pl.ds(start, share), :]

    own_tap = 2 + group
    far_tap = 3 - group
    passes = ((0, 2, zs0, zr0, xs0, xr0, cs0, cr0), (own_tap, 1, zs1, zr1, xs1, xr1, cs1, cr1))

    def column(j):
        return zf[j % 4], (x if j < 4 else 1 - x)

    def z_copy(p, d):
        first, count, send, recv = passes[p][:4]
        return copy_to(slab(first, count, z, x), slab(first, count, z, x),
                       send.at[d], recv.at[d], index(zt[d], x, core))

    def x_copy(p, j):
        first, count, _, _, send, recv = passes[p][:6]
        place_ = slab(first, count, zf[j], x)
        return copy_to(place_, place_,
                       send.at[j], recv.at[j], across)

    def core_copy(p, j):
        first, count, _, _, _, _, send, recv = passes[p]
        if j == 0:
            return copy_to(slab(2 * p, 2, z, x), slab(2 * p, 2, z, x),
                           send.at[0], recv.at[0], other)
        place_ = slab(first, count, *column(j))
        return copy_to(place_, place_, send.at[j], recv.at[j], other)

    def y_copy(j):
        place_ = slab(own_tap, 1, *column(j))
        return pltpu.make_async_remote_copy(
            src_ref=place_, dst_ref=place_, send_sem=ys.at[j], recv_sem=yr.at[j],
            device_id={"groups": 1 - group, "seq": me}, device_id_type=MESH,
        )

    def relay_copy(j):
        place_ = slab(far_tap, 1, *column(j))
        return copy_to(place_, place_, fs.at[j], fr.at[j], other)

    def begin(p):
        for d in (1, 3, 2):
            z_copy(p, d).start()
        x_copy(p, 0).start()
        core_copy(p, 0).start()

    def take_z(p, j):
        z_copy(p, j).wait_recv()
        x_copy(p, j).start()
        core_copy(p, j).start()
        if p == 1:
            y_copy(j).start()

    def take_x(p, j):
        x_copy(p, j).wait_recv()
        core_copy(p, 4 + j).start()
        if p == 1:
            y_copy(4 + j).start()

    n = acted_ref.shape[0] // CHUNKS

    def rows(i):
        return pl.ds(pl.multiple_of(i * n, n), n)

    def halo_z(i):
        return copy_to(out_a.at[i], in_a.at[i], hzs.at[i], hzr.at[i], ahead)

    def halo_x(i):
        return copy_to(out_s.at[i], in_s.at[i], hxs.at[i], hxr.at[i], across)

    for load in loads:
        load.wait()
    begin(0)
    x_load.wait()
    tile = 64

    def act(i, carry):
        r = pl.ds(pl.multiple_of(i * tile, tile), tile)
        v = x_ref[r, :].astype(F32)
        t = jnp.tanh(COEF * (v + CUBE * v * v * v))
        acted_ref[r, :] = (0.5 * v * (1.0 + t)).astype(BF16)
        return carry

    lax.fori_loop(0, x_ref.shape[0] // tile, act, 0)
    acted_store = pltpu.make_async_copy(acted_ref, acted_hbm, own_sem.at[6])
    acted_store.start()
    take_z(0, 1)
    take_z(0, 3)
    take_x(0, 0)
    take_z(0, 2)
    begin(1)
    take_x(0, 1)
    take_x(0, 3)
    take_x(0, 2)
    cot_load.wait()
    for j in range(8):
        core_copy(0, j).wait_recv()

    def far(i, carry):
        out_a[i] = jnp.dot(acted_ref[rows(i), :], w_buf[1 - x], preferred_element_type=F32).astype(BF16)

        @pl.when(sends)
        def _():
            halo_z(i).start()
        return carry

    lax.fori_loop(0, CHUNKS, far, 0)
    take_z(1, 1)
    take_z(1, 3)
    take_x(1, 0)

    def near(i, carry):
        part[i] = jnp.dot(acted_ref[rows(i), :], w_buf[x], preferred_element_type=F32)
        return carry

    lax.fori_loop(0, CHUNKS, near, 0)
    take_z(1, 2)

    def combine(i):
        @pl.when(takes)
        def _():
            halo_z(i).wait_recv()
            part[i] = part[i] + in_a[i].astype(F32)
        out_s[i] = part[i].astype(BF16)
        halo_x(i).start()

    combine(0)
    take_x(1, 1)
    take_x(1, 3)
    combine(1)
    take_x(1, 2)
    combine(2)
    for j in (1, 3, 4, 2, 5, 7, 6):
        y_copy(j).wait_recv()
        relay_copy(j).start()
    combine(3)
    for j in range(8):
        core_copy(1, j).wait_recv()
    for j in range(1, 8):
        relay_copy(j).wait_recv()
    keep = pltpu.make_async_copy(w_buf, full_hbm, own_sem.at[7])
    keep.start()

    def middle(i, carry):
        part[i] = jnp.dot(acted_ref[rows(i), :], w_buf[2], preferred_element_type=F32)
        gg[i] = jnp.dot(cot_ref[rows(i), :], w_buf[3], preferred_element_type=F32)
        return carry

    lax.fori_loop(0, CHUNKS, middle, 0)

    def finish(i, carry):
        halo_x(i).wait_recv()
        hidden = part[i] + in_s[i].astype(F32)
        value, slope = gelu_parts(hidden)
        gated_ref[rows(i), :] = value.astype(BF16)
        hg_ref[rows(i), :] = (gg[i] * slope).astype(BF16)
        return carry

    lax.fori_loop(0, CHUNKS, finish, 0)
    for p in range(2):
        for d in (1, 2, 3):
            z_copy(p, d).wait_send()
        for j in range(4):
            x_copy(p, j).wait_send()
        for j in range(8):
            core_copy(p, j).wait_send()
    for j in range(1, 8):
        y_copy(j).wait_send()
        relay_copy(j).wait_send()
    for i in range(CHUNKS):
        halo_x(i).wait_send()

    @pl.when(sends)
    def _():
        for i in range(CHUNKS):
            halo_z(i).wait_send()

    keep.wait()
    acted_store.wait()


def forward(conv_weight, proj_weight, flat, cot):
    taps, share, hid = 4, proj_weight.shape[0], proj_weight.shape[1]
    m = flat.shape[0]
    dma = pltpu.SemaphoreType.DMA
    block = (CHUNKS, m // CHUNKS, hid)
    full = jax.ShapeDtypeStruct((taps, share * SEQ, hid), BF16)
    return pl.pallas_call(
        forward_kernel,
        out_shape=(full, jax.ShapeDtypeStruct(flat.shape, BF16))
        + (jax.ShapeDtypeStruct((m, hid), BF16),) * 2,
        in_specs=[HBM] * 4,
        out_specs=(HBM, HBM, VMEM, VMEM),
        scratch_shapes=[pltpu.VMEM(full.shape, BF16)] + [pltpu.VMEM(flat.shape, BF16)] * 3
        + [pltpu.VMEM(block, BF16)] * 4 + [pltpu.VMEM(block, F32)] * 2
        + [dma((8,))] + ([dma((4,))] * 4 + [dma((8,))] * 2) * 2
        + [dma((8,))] * 4 + [dma((CHUNKS,))] * 4,
        compiler_params=params(1),
        name="gather_and_forward_halo",
    )(conv_weight, proj_weight, flat, cot)


ORDER = (2, 1, 3, 0)
PASSES = ((1, 3), (0, 2))
NT = (((1,), (1,)), ((), ()))
TN = (((0,), (0,)), ((), ()))


def backward_kernel(scale, hg_ref, acted_hbm, cot_hbm, gated_hbm, x_hbm, w_hbm,
                    grads_ref, outputs_hbm, input_grad_hbm,
                    acted_ref, cot_ref, gated_ref, x_buf, w_buf, o_buf, g_buf, near, give, keep, got, acc,
                    x_out, x_in, z_out, z_in, load, store,
                    hzs, hzr, hxs, hxr, cs, cr, xs, xr, zs, zr, free):
    z, x, core = place()
    share = grads_ref.shape[1]
    zt = [lax.rem(z + d, 4) for d in range(4)]
    across = index(z, 1 - x, core)
    other = index(z, x, 1 - core)
    even = x == 0
    sends = jnp.logical_or(jnp.logical_and(even, z < 3), jnp.logical_and(x == 1, z > 0))
    takes = jnp.logical_or(jnp.logical_and(even, z > 0), jnp.logical_and(x == 1, z < 3))
    ahead = index(lax.rem(z + (1 - 2 * x) + 4, 4), x, core)
    w_load = pltpu.make_async_copy(w_hbm, w_buf, load.at[0])
    x_load = pltpu.make_async_copy(x_hbm, x_buf, load.at[1])
    early = [
        pltpu.make_async_copy(src, dst, load.at[2 + i])
        for i, (src, dst) in enumerate(
            ((acted_hbm, acted_ref), (cot_hbm, cot_ref), (gated_hbm, gated_ref))
        )
    ]
    for copy in early:
        copy.start()
    w_load.start()
    x_load.start()
    greet([index(zt[d], x, core) for d in (1, 2, 3)] + [across, other])
    wide = 4 * share
    tile = 256
    m, hid = hg_ref.shape
    chans = acted_ref.shape[1]
    n = m // CHUNKS

    def rows(i):
        return pl.ds(pl.multiple_of(i * n, n), n)

    half = m // HALO

    def piece(i):
        return pl.ds(i * half, half)

    def halo_x(i):
        return copy_to(hg_ref.at[piece(i), :], near.at[0, piece(i), :], hxs.at[i], hxr.at[i], across)

    def halo_z(i):
        return copy_to(near.at[0, piece(i), :], near.at[1, piece(i), :], hzs.at[i], hzr.at[i], ahead)

    def core_copy(s):
        return copy_to(give.at[s % 2], got.at[s % 2], cs.at[s], cr.at[s], other)

    def x_copy(s):
        return copy_to(x_out.at[s], x_in.at[s], xs.at[s], xr.at[s], across)

    def z_copy(s):
        j = s // 4 * 3 + s % 4
        target = index(zt[ORDER[s % 4]], x, core)
        return copy_to(z_out.at[j], z_in.at[j], zs.at[j], zr.at[j], target)

    def onward(i):
        halo_x(i).wait_recv()

        @pl.when(sends)
        def _():
            halo_z(i).start()

    def compute(s):
        if s >= 2:
            core_copy(s - 2).wait_send()
        cols = pl.ds(pl.multiple_of(zt[ORDER[s % 4]] * wide, wide), wide)
        for j, k in enumerate(PASSES[s // 4]):
            left = cot_ref if k == 3 else acted_ref

            def part(i, carry, k=k, j=j, left=left):
                t = pl.ds(pl.multiple_of(i * tile, tile), tile)
                if k == 3:
                    right = gated_ref[:, t]
                elif k == 1:
                    right = hg_ref[:, t]
                else:
                    right = near[x if k == 0 else 1 - x, :, t]
                p = lax.dot_general(left[:, cols], right, TN, preferred_element_type=F32)
                for xx in range(2):
                    lo = p[2 * xx * share:(2 * xx + 1) * share]
                    hi = p[(2 * xx + 1) * share:(2 * xx + 2) * share]
                    keep[s % 2, xx, j, :, t] = jnp.where(core == 0, lo, hi)
                    give[s % 2, xx, j, :, t] = jnp.where(core == 0, hi, lo)
                return carry

            lax.fori_loop(0, hid // tile, part, 0)
        if s >= 2:
            pl.semaphore_wait(free, 1)
        core_copy(s).start()

    def to_across(s):
        core_copy(s).wait_recv()

        def add(j, carry):
            x_out[s, j] = (keep[s % 2, 1 - x, j] + got[s % 2, 1 - x, j]).astype(BF16)
            acc[s, j] = keep[s % 2, x, j] + got[s % 2, x, j]
            return carry

        lax.fori_loop(0, 2, add, 0)
        x_copy(s).start()
        if s < 6:
            pl.semaphore_signal(free, inc=1, device_id={"seq": other}, device_id_type=MESH)

    def to_z(s):
        x_copy(s).wait_recv()
        for j in range(2):
            z_out[s // 4 * 3 + s % 4, j] = (acc[s, j] + x_in[s, j].astype(F32)).astype(BF16)
        z_copy(s).start()

    span = 512

    def out_store(i):
        return pltpu.make_async_copy(o_buf.at[rows(i), :], outputs_hbm.at[rows(i), :], store.at[i])

    def grad_store(i):
        return pltpu.make_async_copy(
            g_buf.at[rows(i), :], input_grad_hbm.at[rows(i), :], store.at[CHUNKS + i]
        )

    def project(i, carry):
        def part(j, c):
            t = pl.ds(pl.multiple_of(j * span, span), span)
            p = lax.dot_general(gated_ref[rows(i), :], w_buf[3, t, :], NT, preferred_element_type=F32)
            o_buf[rows(i), t] = (x_buf[rows(i), t].astype(F32) + p).astype(BF16)
            return c

        lax.fori_loop(0, chans // span, part, 0)
        out_store(i).start()
        return carry

    def spread(i, carry):
        def part(j, c):
            t = pl.ds(pl.multiple_of(j * span, span), span)
            p = lax.dot_general(hg_ref[rows(i), :], w_buf[2, t, :], NT, preferred_element_type=F32)
            p += lax.dot_general(near[x, rows(i), :], w_buf[0, t, :], NT, preferred_element_type=F32)
            p += lax.dot_general(near[1 - x, rows(i), :], w_buf[1, t, :], NT, preferred_element_type=F32)
            slope = gelu_parts(x_buf[rows(i), t].astype(F32))[1]
            g_buf[rows(i), t] = (cot_ref[rows(i), t].astype(F32) + p * slope).astype(BF16)
            return c

        lax.fori_loop(0, chans // span, part, 0)
        grad_store(i).start()
        return carry

    for i in range(HALO):
        halo_x(i).start()

    @pl.when(jnp.logical_not(takes))
    def _():
        near[1] = jnp.zeros((m, hid), BF16)

    for copy in early:
        copy.wait()
    compute(0)
    compute(1)
    onward(0)
    onward(1)
    onward(2)
    onward(3)
    w_load.wait()
    x_load.wait()
    lax.fori_loop(0, 2, project, 0)
    onward(4)
    onward(5)
    to_across(0)
    compute(2)
    onward(6)
    onward(7)
    to_across(1)
    compute(3)
    to_across(2)
    to_across(3)
    lax.fori_loop(2, CHUNKS, project, 0)
    to_z(0)

    @pl.when(takes)
    def _():
        for i in range(HALO):
            halo_z(i).wait_recv()

    compute(4)
    to_z(1)
    compute(5)
    to_across(4)
    to_z(2)
    compute(6)
    to_across(5)
    compute(7)
    to_across(6)
    to_across(7)
    to_z(4)
    lax.fori_loop(0, 2, spread, 0)
    to_z(5)
    lax.fori_loop(2, CHUNKS, spread, 0)
    to_z(6)
    for s in (3, 7):
        x_copy(s).wait_recv()
        for j in range(s // 4 * 3, s // 4 * 3 + 3):
            z_copy(s // 4 * 4 + j % 3).wait_recv()
        for j in range(2):
            own = acc[s, j] + x_in[s, j].astype(F32)
            for i in range(s // 4 * 3, s // 4 * 3 + 3):
                own = own + z_in[i, j].astype(F32)
            grads_ref[PASSES[s // 4][j]] = own * scale
    for i in range(CHUNKS):
        out_store(i).wait()
        grad_store(i).wait()
    for i in range(HALO):
        halo_x(i).wait_send()

    @pl.when(sends)
    def _():
        for i in range(HALO):
            halo_z(i).wait_send()

    core_copy(6).wait_send()
    core_copy(7).wait_send()
    for s in range(8):
        x_copy(s).wait_send()
        if s % 4 < 3:
            z_copy(s).wait_send()


def backward(scale, hg, acted, cot, gated, rows, full):
    m, hid = hg.shape
    chans = acted.shape[1]
    share = chans // SEQ
    dma = pltpu.SemaphoreType.DMA
    pair = (2, 2, share, hid)
    return pl.pallas_call(
        functools.partial(backward_kernel, scale),
        out_shape=(
            jax.ShapeDtypeStruct((4, share, hid), F32),
            jax.ShapeDtypeStruct((m, chans), BF16),
            jax.ShapeDtypeStruct((m, chans), BF16),
        ),
        in_specs=[VMEM] + [HBM] * 5,
        out_specs=(VMEM, HBM, HBM),
        scratch_shapes=[
            pltpu.VMEM((m, chans), BF16),
            pltpu.VMEM((m, chans), BF16),
            pltpu.VMEM((m, hid), BF16),
            pltpu.VMEM((m, chans), BF16),
            pltpu.VMEM(full.shape, BF16),
            pltpu.VMEM((m, chans), BF16),
            pltpu.VMEM((m, chans), BF16),
            pltpu.VMEM((2, m, hid), BF16),
            pltpu.VMEM((2,) + pair, F32),
            pltpu.VMEM((2,) + pair, F32),
            pltpu.VMEM((2,) + pair, F32),
            pltpu.VMEM((8, 2, share, hid), F32),
            pltpu.VMEM((8, 2, share, hid), BF16),
            pltpu.VMEM((8, 2, share, hid), BF16),
            pltpu.VMEM((6, 2, share, hid), BF16),
            pltpu.VMEM((6, 2, share, hid), BF16),
            dma((5,)), dma((2 * CHUNKS,)),
            dma((HALO,)), dma((HALO,)), dma((HALO,)), dma((HALO,)),
            dma((8,)), dma((8,)), dma((8,)), dma((8,)), dma((6,)), dma((6,)),
            pltpu.SemaphoreType.REGULAR,
        ],
        compiler_params=params(2, 62),
        name="backward_halo_and_reduce",
    )(hg, acted, cot, gated, rows, full)


def pair_shards(inputs, conv_weight, proj_weight, cotangent):
    batch, local_len, chans = inputs.shape
    scale = 1.0 / float(batch * L) ** 0.5
    rows = inputs.reshape(-1, chans)
    cot = cotangent.reshape(-1, chans)
    full, acted, gated, hg = forward(conv_weight, proj_weight, rows, cot)
    grads, outputs, input_grad = backward(scale, hg, acted, cot, gated, rows, full)
    return (
        outputs.reshape(batch, local_len, chans),
        input_grad.reshape(batch, local_len, chans),
        grads[:3].transpose(1, 0, 2),
        grads[3],
    )


def solution(mesh):
    fast = mesh.shape["seq"] == SEQ
    return jax.shard_map(
        pair_shards if fast else shards,
        mesh=mesh,
        in_specs=(
            P("groups", "seq", None),
            P(None, "seq", None),
            P("seq", None),
            P("groups", "seq", None),
        ),
        out_specs=(
            P("groups", "seq", None),
            P("groups", "seq", None),
            P(("groups", "seq"), None, None),
            P(("groups", "seq"), None),
        ),
        check_vma=False,
    )
```

```python
import functools

import jax
import jax.numpy as jnp
from jax import lax
from jax.experimental import pallas as pl
from jax.experimental.pallas import tpu as pltpu
from jax.sharding import PartitionSpec as P

L = 8192


def from_behind(block, axis, distance):
    devices = range(lax.axis_size(axis))
    route = [(i - distance, i) for i in devices if i - distance in devices]
    return lax.ppermute(block, axis, route)


def gelu_grad(point, upstream):
    return jax.vjp(jax.nn.gelu, point)[1](upstream)[0]


def shards(inputs, conv_weight, proj_weight, cotangent):
    batch, local_len, chans = inputs.shape
    devices = lax.axis_size("seq")
    stride = devices // 8
    scale = 1.0 / float(batch * L) ** 0.5
    acted = jax.nn.gelu(inputs.astype(jnp.float32)).astype(jnp.bfloat16)
    conv_weight, proj_weight = (
        lax.all_gather(conv_weight, "seq", axis=1, tiled=True),
        lax.all_gather(proj_weight, "seq", axis=0, tiled=True),
    )
    hid = conv_weight.shape[2]
    acted_rows = acted.reshape(-1, chans)
    before = from_behind(acted, "seq", stride)
    after = from_behind(acted, "seq", -stride)
    hidden = jnp.dot(before.reshape(-1, chans), conv_weight[0], preferred_element_type=jnp.float32)
    hidden = hidden + jnp.dot(acted_rows, conv_weight[1], preferred_element_type=jnp.float32)
    hidden = hidden + jnp.dot(
        after.reshape(-1, chans), conv_weight[2], preferred_element_type=jnp.float32
    )
    gated = jax.nn.gelu(hidden).astype(jnp.bfloat16)
    outputs = (
        inputs.reshape(-1, chans).astype(jnp.float32)
        + jnp.dot(gated, proj_weight.T, preferred_element_type=jnp.float32)
    ).astype(jnp.bfloat16)
    cot_rows = cotangent.reshape(-1, chans)
    gated_grad = jnp.dot(cot_rows, proj_weight, preferred_element_type=jnp.float32)
    hidden_grad = gelu_grad(hidden, gated_grad).astype(jnp.bfloat16)
    grad_blocks = hidden_grad.reshape(batch, local_len, hid)
    grad_later = from_behind(grad_blocks, "seq", -stride).reshape(-1, hid)
    grad_earlier = from_behind(grad_blocks, "seq", stride).reshape(-1, hid)
    acted_grad = jnp.dot(grad_later, conv_weight[0].T, preferred_element_type=jnp.float32)
    acted_grad = acted_grad + jnp.dot(
        hidden_grad, conv_weight[1].T, preferred_element_type=jnp.float32
    )
    acted_grad = acted_grad + jnp.dot(
        grad_earlier, conv_weight[2].T, preferred_element_type=jnp.float32
    )
    input_grad = (
        cot_rows.astype(jnp.float32)
        + gelu_grad(inputs.reshape(-1, chans).astype(jnp.float32), acted_grad)
    ).astype(jnp.bfloat16)
    tap_grads = (grad_later, hidden_grad, grad_earlier)
    share = chans // devices
    local_terms = [
        jnp.dot(acted_rows.T, piece, preferred_element_type=jnp.float32) for piece in tap_grads
    ]
    local_terms.append(jnp.dot(cot_rows.T, gated, preferred_element_type=jnp.float32))
    stacked = jnp.stack(local_terms, axis=1)
    received = lax.all_to_all(stacked, "seq", split_axis=0, concat_axis=0, tiled=True)
    summed = jnp.sum(received.reshape(devices, share, 4, received.shape[2]), axis=0)
    conv_sum = summed[:, 0:3, :]
    proj_sum = summed[:, 3, :]
    return (
        outputs.reshape(batch, local_len, chans),
        input_grad.reshape(batch, local_len, chans),
        conv_sum * scale,
        proj_sum * scale,
    )


F32 = jnp.float32
BF16 = jnp.bfloat16
MESH = pl.DeviceIdType.MESH
VMEM = pl.BlockSpec(memory_space=pltpu.VMEM)
HBM = pl.BlockSpec(memory_space=pl.ANY)
SEQ = 16
CHUNKS = 4
HALO = 8
COEF = 0.7978845608028654
CUBE = 0.044715


def place():
    s = lax.axis_index("seq")
    return s // 4, (s // 2) % 2, s % 2


def index(z, x, core):
    return (z * 2 + x) * 2 + core


def copy_to(src, dst, send, recv, target):
    return pltpu.make_async_remote_copy(
        src_ref=src, dst_ref=dst, send_sem=send, recv_sem=recv,
        device_id={"seq": target}, device_id_type=MESH,
    )


def greet(targets):
    barrier = pltpu.get_barrier_semaphore()
    for target in targets:
        pl.semaphore_signal(barrier, inc=1, device_id={"seq": target}, device_id_type=MESH)
    pl.semaphore_wait(barrier, len(targets))


def gelu_parts(v):
    t = jnp.tanh(COEF * (v + CUBE * v * v * v))
    half = 0.5 * (1.0 + t)
    return half * v, half + (0.5 * COEF) * v * (1.0 - t * t) * (1.0 + (3.0 * CUBE) * v * v)


def params(cid, mib=56):
    return pltpu.CompilerParams(
        collective_id=cid, has_side_effects=True, vmem_limit_bytes=mib * 1024 * 1024
    )


def forward_kernel(conv_hbm, proj_hbm, x_hbm, cot_hbm, full_hbm, acted_hbm, gated_ref, hg_ref,
                   w_buf, x_ref, cot_ref, acted_ref, out_a, in_a, out_s, in_s, part, gg, own_sem,
                   zs0, zr0, xs0, xr0, cs0, cr0, zs1, zr1, xs1, xr1, cs1, cr1,
                   ys, yr, fs, fr, hzs, hzr, hxs, hxr):
    z, x, core = place()
    group = lax.axis_index("groups")
    me = lax.axis_index("seq")
    share = proj_hbm.shape[0]
    zt = [lax.rem(z + d, 4) for d in range(4)]
    zf = [lax.rem(z + 4 - d, 4) for d in range(4)]
    across = index(z, 1 - x, core)
    other = index(z, x, 1 - core)
    up = x == 1
    sends = jnp.logical_or(jnp.logical_and(up, z < 3), jnp.logical_and(x == 0, z > 0))
    takes = jnp.logical_or(jnp.logical_and(up, z > 0), jnp.logical_and(x == 0, z < 3))
    ahead = index(lax.rem(z + (2 * x - 1) + 4, 4), x, core)

    mine = pl.ds(pl.multiple_of(me * share, share), share)
    loads = [
        pltpu.make_async_copy(conv_hbm.at[tap], w_buf.at[slot, mine, :], own_sem.at[slot])
        for slot, tap in enumerate((0, 2, 1))
    ]
    loads.append(pltpu.make_async_copy(proj_hbm, w_buf.at[3, mine, :], own_sem.at[3]))
    x_load = pltpu.make_async_copy(x_hbm, x_ref, own_sem.at[4])
    cot_load = pltpu.make_async_copy(cot_hbm, cot_ref, own_sem.at[5])
    for load in loads:
        load.start()
    x_load.start()
    cot_load.start()
    barrier = pltpu.get_barrier_semaphore()
    for target in [index(zt[d], x, core) for d in (1, 2, 3)] + [across, other]:
        pl.semaphore_signal(barrier, inc=1, device_id={"seq": target}, device_id_type=MESH)
    pl.semaphore_signal(
        barrier, inc=1, device_id={"groups": 1 - group, "seq": me}, device_id_type=MESH
    )
    pl.semaphore_wait(barrier, 6)

    def slab(first, count, zz, xx):
        start = pl.multiple_of(index(zz, xx, core) * share, share)
        return w_buf.at[pl.ds(first, count), pl.ds(start, share), :]

    own_tap = 2 + group
    far_tap = 3 - group
    passes = ((0, 2, zs0, zr0, xs0, xr0, cs0, cr0), (own_tap, 1, zs1, zr1, xs1, xr1, cs1, cr1))

    def column(j):
        return zf[j % 4], (x if j < 4 else 1 - x)

    def z_copy(p, d):
        first, count, send, recv = passes[p][:4]
        return copy_to(slab(first, count, z, x), slab(first, count, z, x),
                       send.at[d], recv.at[d], index(zt[d], x, core))

    def x_copy(p, j):
        first, count, _, _, send, recv = passes[p][:6]
        place_ = slab(first, count, zf[j], x)
        return copy_to(place_, place_,
                       send.at[j], recv.at[j], across)

    def core_copy(p, j):
        first, count, _, _, _, _, send, recv = passes[p]
        if j == 0:
            return copy_to(slab(2 * p, 2, z, x), slab(2 * p, 2, z, x),
                           send.at[0], recv.at[0], other)
        place_ = slab(first, count, *column(j))
        return copy_to(place_, place_, send.at[j], recv.at[j], other)

    def y_copy(j):
        place_ = slab(own_tap, 1, *column(j))
        return pltpu.make_async_remote_copy(
            src_ref=place_, dst_ref=place_, send_sem=ys.at[j], recv_sem=yr.at[j],
            device_id={"groups": 1 - group, "seq": me}, device_id_type=MESH,
        )

    def relay_copy(j):
        place_ = slab(far_tap, 1, *column(j))
        return copy_to(place_, place_, fs.at[j], fr.at[j], other)

    def begin(p):
        for d in (1, 3, 2):
            z_copy(p, d).start()
        x_copy(p, 0).start()
        core_copy(p, 0).start()

    def take_z(p, j):
        z_copy(p, j).wait_recv()
        x_copy(p, j).start()
        core_copy(p, j).start()
        if p == 1:
            y_copy(j).start()

    def take_x(p, j):
        x_copy(p, j).wait_recv()
        core_copy(p, 4 + j).start()
        if p == 1:
            y_copy(4 + j).start()

    n = acted_ref.shape[0] // CHUNKS

    def rows(i):
        return pl.ds(pl.multiple_of(i * n, n), n)

    def halo_z(i):
        return copy_to(out_a.at[i], in_a.at[i], hzs.at[i], hzr.at[i], ahead)

    def halo_x(i):
        return copy_to(out_s.at[i], in_s.at[i], hxs.at[i], hxr.at[i], across)

    for load in loads:
        load.wait()
    begin(0)
    x_load.wait()
    tile = 64

    def act(i, carry):
        r = pl.ds(pl.multiple_of(i * tile, tile), tile)
        v = x_ref[r, :].astype(F32)
        t = jnp.tanh(COEF * (v + CUBE * v * v * v))
        acted_ref[r, :] = (0.5 * v * (1.0 + t)).astype(BF16)
        return carry

    lax.fori_loop(0, x_ref.shape[0] // tile, act, 0)
    acted_store = pltpu.make_async_copy(acted_ref, acted_hbm, own_sem.at[6])
    acted_store.start()
    take_z(0, 1)
    take_z(0, 3)
    take_x(0, 0)
    take_z(0, 2)
    begin(1)
    take_x(0, 1)
    take_x(0, 3)
    take_x(0, 2)
    cot_load.wait()
    for j in range(8):
        core_copy(0, j).wait_recv()

    def far(i, carry):
        out_a[i] = jnp.dot(acted_ref[rows(i), :], w_buf[1 - x], preferred_element_type=F32).astype(BF16)

        @pl.when(sends)
        def _():
            halo_z(i).start()
        return carry

    lax.fori_loop(0, CHUNKS, far, 0)
    take_z(1, 1)
    take_z(1, 3)
    take_x(1, 0)

    def near(i, carry):
        part[i] = jnp.dot(acted_ref[rows(i), :], w_buf[x], preferred_element_type=F32)
        return carry

    lax.fori_loop(0, CHUNKS, near, 0)
    take_z(1, 2)

    def combine(i):
        @pl.when(takes)
        def _():
            halo_z(i).wait_recv()
            part[i] = part[i] + in_a[i].astype(F32)
        out_s[i] = part[i].astype(BF16)
        halo_x(i).start()

    combine(0)
    take_x(1, 1)
    take_x(1, 3)
    combine(1)
    take_x(1, 2)
    combine(2)
    for j in (1, 3, 4, 2, 5, 7, 6):
        y_copy(j).wait_recv()
        relay_copy(j).start()
    for j in range(8):
        core_copy(1, j).wait_recv()
    for j in range(1, 8):
        relay_copy(j).wait_recv()
    keep = pltpu.make_async_copy(w_buf, full_hbm, own_sem.at[7])
    keep.start()

    def middle(i, carry):
        part[i] = jnp.dot(acted_ref[rows(i), :], w_buf[2], preferred_element_type=F32)
        gg[i] = jnp.dot(cot_ref[rows(i), :], w_buf[3], preferred_element_type=F32)
        return carry

    lax.fori_loop(0, CHUNKS - 1, middle, 0)
    combine(CHUNKS - 1)
    lax.fori_loop(CHUNKS - 1, CHUNKS, middle, 0)

    def finish(i, carry):
        halo_x(i).wait_recv()
        hidden = part[i] + in_s[i].astype(F32)
        value, slope = gelu_parts(hidden)
        gated_ref[rows(i), :] = value.astype(BF16)
        hg_ref[rows(i), :] = (gg[i] * slope).astype(BF16)
        return carry

    lax.fori_loop(0, CHUNKS, finish, 0)
    for p in range(2):
        for d in (1, 2, 3):
            z_copy(p, d).wait_send()
        for j in range(4):
            x_copy(p, j).wait_send()
        for j in range(8):
            core_copy(p, j).wait_send()
    for j in range(1, 8):
        y_copy(j).wait_send()
        relay_copy(j).wait_send()
    for i in range(CHUNKS):
        halo_x(i).wait_send()

    @pl.when(sends)
    def _():
        for i in range(CHUNKS):
            halo_z(i).wait_send()

    keep.wait()
    acted_store.wait()


def forward(conv_weight, proj_weight, flat, cot):
    taps, share, hid = 4, proj_weight.shape[0], proj_weight.shape[1]
    m = flat.shape[0]
    dma = pltpu.SemaphoreType.DMA
    block = (CHUNKS, m // CHUNKS, hid)
    full = jax.ShapeDtypeStruct((taps, share * SEQ, hid), BF16)
    return pl.pallas_call(
        forward_kernel,
        out_shape=(full, jax.ShapeDtypeStruct(flat.shape, BF16))
        + (jax.ShapeDtypeStruct((m, hid), BF16),) * 2,
        in_specs=[HBM] * 4,
        out_specs=(HBM, HBM, VMEM, VMEM),
        scratch_shapes=[pltpu.VMEM(full.shape, BF16)] + [pltpu.VMEM(flat.shape, BF16)] * 3
        + [pltpu.VMEM(block, BF16)] * 4 + [pltpu.VMEM(block, F32)] * 2
        + [dma((8,))] + ([dma((4,))] * 4 + [dma((8,))] * 2) * 2
        + [dma((8,))] * 4 + [dma((CHUNKS,))] * 4,
        compiler_params=params(1),
        name="gather_and_forward_halo",
    )(conv_weight, proj_weight, flat, cot)


ORDER = (2, 1, 3, 0)
PASSES = ((1, 3), (0, 2))
NT = (((1,), (1,)), ((), ()))
TN = (((0,), (0,)), ((), ()))


def backward_kernel(scale, hg_ref, acted_hbm, cot_hbm, gated_hbm, x_hbm, w_hbm,
                    grads_ref, outputs_hbm, input_grad_hbm,
                    acted_ref, cot_ref, gated_ref, x_buf, w_buf, o_buf, g_buf, near, give, keep, got, acc,
                    x_out, x_in, z_out, z_in, load, store,
                    hzs, hzr, hxs, hxr, cs, cr, xs, xr, zs, zr, free):
    z, x, core = place()
    share = grads_ref.shape[1]
    zt = [lax.rem(z + d, 4) for d in range(4)]
    across = index(z, 1 - x, core)
    other = index(z, x, 1 - core)
    even = x == 0
    sends = jnp.logical_or(jnp.logical_and(even, z < 3), jnp.logical_and(x == 1, z > 0))
    takes = jnp.logical_or(jnp.logical_and(even, z > 0), jnp.logical_and(x == 1, z < 3))
    ahead = index(lax.rem(z + (1 - 2 * x) + 4, 4), x, core)
    w_load = pltpu.make_async_copy(w_hbm, w_buf, load.at[0])
    x_load = pltpu.make_async_copy(x_hbm, x_buf, load.at[1])
    early = [
        pltpu.make_async_copy(src, dst, load.at[2 + i])
        for i, (src, dst) in enumerate(
            ((acted_hbm, acted_ref), (cot_hbm, cot_ref), (gated_hbm, gated_ref))
        )
    ]
    for copy in early:
        copy.start()
    w_load.start()
    x_load.start()
    greet([index(zt[d], x, core) for d in (1, 2, 3)] + [across, other])
    wide = 4 * share
    tile = 256
    m, hid = hg_ref.shape
    chans = acted_ref.shape[1]
    n = m // CHUNKS

    def rows(i):
        return pl.ds(pl.multiple_of(i * n, n), n)

    half = m // HALO

    def piece(i):
        return pl.ds(i * half, half)

    def halo_x(i):
        return copy_to(hg_ref.at[piece(i), :], near.at[0, piece(i), :], hxs.at[i], hxr.at[i], across)

    def halo_z(i):
        return copy_to(near.at[0, piece(i), :], near.at[1, piece(i), :], hzs.at[i], hzr.at[i], ahead)

    def core_copy(s):
        return copy_to(give.at[s % 2], got.at[s % 2], cs.at[s], cr.at[s], other)

    def x_copy(s):
        return copy_to(x_out.at[s], x_in.at[s], xs.at[s], xr.at[s], across)

    def z_copy(s):
        j = s // 4 * 3 + s % 4
        target = index(zt[ORDER[s % 4]], x, core)
        return copy_to(z_out.at[j], z_in.at[j], zs.at[j], zr.at[j], target)

    def onward(i):
        halo_x(i).wait_recv()

        @pl.when(sends)
        def _():
            halo_z(i).start()

    def compute(s):
        if s >= 2:
            core_copy(s - 2).wait_send()
        cols = pl.ds(pl.multiple_of(zt[ORDER[s % 4]] * wide, wide), wide)
        for j, k in enumerate(PASSES[s // 4]):
            left = cot_ref if k == 3 else acted_ref

            def part(i, carry, k=k, j=j, left=left):
                t = pl.ds(pl.multiple_of(i * tile, tile), tile)
                if k == 3:
                    right = gated_ref[:, t]
                elif k == 1:
                    right = hg_ref[:, t]
                else:
                    right = near[x if k == 0 else 1 - x, :, t]
                p = lax.dot_general(left[:, cols], right, TN, preferred_element_type=F32)
                for xx in range(2):
                    lo = p[2 * xx * share:(2 * xx + 1) * share]
                    hi = p[(2 * xx + 1) * share:(2 * xx + 2) * share]
                    keep[s % 2, xx, j, :, t] = jnp.where(core == 0, lo, hi)
                    give[s % 2, xx, j, :, t] = jnp.where(core == 0, hi, lo)
                return carry

            lax.fori_loop(0, hid // tile, part, 0)
        if s >= 2:
            pl.semaphore_wait(free, 1)
        core_copy(s).start()

    def to_across(s):
        core_copy(s).wait_recv()

        def add(j, carry):
            x_out[s, j] = (keep[s % 2, 1 - x, j] + got[s % 2, 1 - x, j]).astype(BF16)
            acc[s, j] = keep[s % 2, x, j] + got[s % 2, x, j]
            return carry

        lax.fori_loop(0, 2, add, 0)
        x_copy(s).start()
        if s < 6:
            pl.semaphore_signal(free, inc=1, device_id={"seq": other}, device_id_type=MESH)

    def to_z(s):
        x_copy(s).wait_recv()
        for j in range(2):
            z_out[s // 4 * 3 + s % 4, j] = (acc[s, j] + x_in[s, j].astype(F32)).astype(BF16)
        z_copy(s).start()

    span = 512

    def out_store(i):
        return pltpu.make_async_copy(o_buf.at[rows(i), :], outputs_hbm.at[rows(i), :], store.at[i])

    def grad_store(i):
        return pltpu.make_async_copy(
            g_buf.at[rows(i), :], input_grad_hbm.at[rows(i), :], store.at[CHUNKS + i]
        )

    def project(i, carry):
        def part(j, c):
            t = pl.ds(pl.multiple_of(j * span, span), span)
            p = lax.dot_general(gated_ref[rows(i), :], w_buf[3, t, :], NT, preferred_element_type=F32)
            o_buf[rows(i), t] = (x_buf[rows(i), t].astype(F32) + p).astype(BF16)
            return c

        lax.fori_loop(0, chans // span, part, 0)
        out_store(i).start()
        return carry

    def spread(i, carry):
        def part(j, c):
            t = pl.ds(pl.multiple_of(j * span, span), span)
            p = lax.dot_general(hg_ref[rows(i), :], w_buf[2, t, :], NT, preferred_element_type=F32)
            p += lax.dot_general(near[x, rows(i), :], w_buf[0, t, :], NT, preferred_element_type=F32)
            p += lax.dot_general(near[1 - x, rows(i), :], w_buf[1, t, :], NT, preferred_element_type=F32)
            slope = gelu_parts(x_buf[rows(i), t].astype(F32))[1]
            g_buf[rows(i), t] = (cot_ref[rows(i), t].astype(F32) + p * slope).astype(BF16)
            return c

        lax.fori_loop(0, chans // span, part, 0)
        grad_store(i).start()
        return carry

    for i in range(HALO):
        halo_x(i).start()

    @pl.when(jnp.logical_not(takes))
    def _():
        near[1] = jnp.zeros((m, hid), BF16)

    for copy in early:
        copy.wait()
    compute(0)
    compute(1)
    onward(0)
    onward(1)
    onward(2)
    onward(3)
    w_load.wait()
    x_load.wait()
    lax.fori_loop(0, 2, project, 0)
    onward(4)
    onward(5)
    to_across(0)
    compute(2)
    onward(6)
    onward(7)
    to_across(1)
    compute(3)
    to_across(2)
    to_across(3)
    lax.fori_loop(2, CHUNKS, project, 0)
    to_z(0)

    @pl.when(takes)
    def _():
        for i in range(HALO):
            halo_z(i).wait_recv()

    compute(4)
    to_z(1)
    compute(5)
    to_across(4)
    to_z(2)
    compute(6)
    to_across(5)
    compute(7)
    to_across(6)
    to_across(7)
    to_z(4)
    lax.fori_loop(0, 2, spread, 0)
    to_z(5)
    lax.fori_loop(2, CHUNKS, spread, 0)
    to_z(6)
    for s in (3, 7):
        x_copy(s).wait_recv()
        for j in range(s // 4 * 3, s // 4 * 3 + 3):
            z_copy(s // 4 * 4 + j % 3).wait_recv()
        for j in range(2):
            own = acc[s, j] + x_in[s, j].astype(F32)
            for i in range(s // 4 * 3, s // 4 * 3 + 3):
                own = own + z_in[i, j].astype(F32)
            grads_ref[PASSES[s // 4][j]] = own * scale
    for i in range(CHUNKS):
        out_store(i).wait()
        grad_store(i).wait()
    for i in range(HALO):
        halo_x(i).wait_send()

    @pl.when(sends)
    def _():
        for i in range(HALO):
            halo_z(i).wait_send()

    core_copy(6).wait_send()
    core_copy(7).wait_send()
    for s in range(8):
        x_copy(s).wait_send()
        if s % 4 < 3:
            z_copy(s).wait_send()


def backward(scale, hg, acted, cot, gated, rows, full):
    m, hid = hg.shape
    chans = acted.shape[1]
    share = chans // SEQ
    dma = pltpu.SemaphoreType.DMA
    pair = (2, 2, share, hid)
    return pl.pallas_call(
        functools.partial(backward_kernel, scale),
        out_shape=(
            jax.ShapeDtypeStruct((4, share, hid), F32),
            jax.ShapeDtypeStruct((m, chans), BF16),
            jax.ShapeDtypeStruct((m, chans), BF16),
        ),
        in_specs=[VMEM] + [HBM] * 5,
        out_specs=(VMEM, HBM, HBM),
        scratch_shapes=[
            pltpu.VMEM((m, chans), BF16),
            pltpu.VMEM((m, chans), BF16),
            pltpu.VMEM((m, hid), BF16),
            pltpu.VMEM((m, chans), BF16),
            pltpu.VMEM(full.shape, BF16),
            pltpu.VMEM((m, chans), BF16),
            pltpu.VMEM((m, chans), BF16),
            pltpu.VMEM((2, m, hid), BF16),
            pltpu.VMEM((2,) + pair, F32),
            pltpu.VMEM((2,) + pair, F32),
            pltpu.VMEM((2,) + pair, F32),
            pltpu.VMEM((8, 2, share, hid), F32),
            pltpu.VMEM((8, 2, share, hid), BF16),
            pltpu.VMEM((8, 2, share, hid), BF16),
            pltpu.VMEM((6, 2, share, hid), BF16),
            pltpu.VMEM((6, 2, share, hid), BF16),
            dma((5,)), dma((2 * CHUNKS,)),
            dma((HALO,)), dma((HALO,)), dma((HALO,)), dma((HALO,)),
            dma((8,)), dma((8,)), dma((8,)), dma((8,)), dma((6,)), dma((6,)),
            pltpu.SemaphoreType.REGULAR,
        ],
        compiler_params=params(2, 62),
        name="backward_halo_and_reduce",
    )(hg, acted, cot, gated, rows, full)


def pair_shards(inputs, conv_weight, proj_weight, cotangent):
    batch, local_len, chans = inputs.shape
    scale = 1.0 / float(batch * L) ** 0.5
    rows = inputs.reshape(-1, chans)
    cot = cotangent.reshape(-1, chans)
    full, acted, gated, hg = forward(conv_weight, proj_weight, rows, cot)
    grads, outputs, input_grad = backward(scale, hg, acted, cot, gated, rows, full)
    return (
        outputs.reshape(batch, local_len, chans),
        input_grad.reshape(batch, local_len, chans),
        grads[:3].transpose(1, 0, 2),
        grads[3],
    )


def solution(mesh):
    fast = mesh.shape["seq"] == SEQ
    return jax.shard_map(
        pair_shards if fast else shards,
        mesh=mesh,
        in_specs=(
            P("groups", "seq", None),
            P(None, "seq", None),
            P("seq", None),
            P("groups", "seq", None),
        ),
        out_specs=(
            P("groups", "seq", None),
            P("groups", "seq", None),
            P(("groups", "seq"), None, None),
            P(("groups", "seq"), None),
        ),
        check_vma=False,
    )
```
